256 devices in a mesh: pipe: 8 (over y_hi, x), dp: 32 (over y_lo, z, core).
Axes of the slice: x: 4, y: 4 (y_hi: 2, y_lo: 2; y = y_hi * 2 + y_lo), z: 8, core: 2. Of those that a mesh axis runs over, the one named last changes fastest.
Arguments:
- new_input: bfloat16 [8, 4096, 8192], P('pipe', 'dp'), may hold values from -400 to 400
- new_gain: bfloat16 [8, 8192], P('pipe'), may hold values from 0.5 to 1.5
- queries: bfloat16 [8, 4096, 4096], P('pipe', 'dp'), may hold values from -5 to 5
- new_keys: bfloat16 [8, 4096, 512], P('pipe', 'dp'), may hold values from -5 to 5
- context_grad: bfloat16 [8, 4096, 4096], P('pipe', 'dp'), may hold values from -0.08984375 to 0.08984375
- segment_ids: int32 [8, 4096], P('pipe', 'dp'), may hold values from 0 to 63, never falling along the last dimension, each value on 1 to 128 neighbouring positions
- frozen_input: bfloat16 [8, 4096, 8192], P('pipe', 'dp'), may hold values from -400 to 400
- frozen_gain: bfloat16 [8, 8192], P('pipe'), may hold values from 0.5 to 1.5
- output_grad: bfloat16 [8, 4096, 8192], P('pipe', 'dp'), may hold values from -6 to 6
- kv_grad: bfloat16 [8, 4096, 1024], P('pipe', 'dp'), may hold values from -18 to 18
- kv_weight: bfloat16 [8, 8192, 1024], P('pipe', 'dp'), may hold values from -0.0625 to 0.0625
Outputs:
- cot_below: bfloat16 [8, 4096, 8192], P('pipe', 'dp')
- value_grad: float32 [8, 8192, 512], P('pipe', 'dp')
The draws below stay inside these ranges and needn't reach their ends.
Inputs may be any that keep to these rules, and one draw needn't show every extreme that they name: `segment_ids`: within a section the numbers never fall; every number of 0 to 63 appears, on 1 to 128 positions in a row, one on exactly 128.
All inputs are finite; a program needn't handle non-finite values.
Results may differ from the reference program's by a relative error of at most 0.0056.
Values may be sent and summed in bfloat16 or wider, within the bound.
A program may use at most 128 MiB of HBM per device.

```python
import math
import jax
import jax.numpy as jnp
import numpy as np
from jax import lax

D = 8192
HEAD = 128
KVHEADS = 4
GROUP = 8
QW = 4096
KVW = 512
TOK_DEV = 128
TOKENS = 4096
SEGS = 64
SECTIONS = 8


def scaled_rows(key, shape):
    key_base, key_rows, key_cols = jax.random.split(key, 3)
    base_vals = jnp.clip(jax.random.normal(key_base, shape, jnp.float32), -4.0, 4.0)
    col_shape = (shape[0], 1, shape[2])
    upper_log = math.log(10.0)
    row_scale = jnp.exp(jax.random.uniform(key_rows, (shape[0], shape[1], 1), jnp.float32, 0.0, upper_log))
    col_scale = jnp.exp(jax.random.uniform(key_cols, col_shape, jnp.float32, 0.0, math.log(4.0)))
    return base_vals * row_scale * col_scale


def draw_new_input(key, part):
    return scaled_rows(jax.random.fold_in(key, 3), (SECTIONS, TOKENS, D)).astype(jnp.bfloat16)


def draw_frozen_input(key, part):
    return scaled_rows(jax.random.fold_in(key, 5), (SECTIONS, TOKENS, D)).astype(jnp.bfloat16)


def drawn_pair(key):
    base_key = jax.random.fold_in(key, 17)
    key_query, key_key = jax.random.split(base_key, 2)
    query_vals = jnp.clip(jax.random.normal(key_query, (SECTIONS, TOKENS, KVHEADS, GROUP, HEAD), jnp.float32), -4.0, 4.0)
    key_vals = jnp.clip(jax.random.normal(key_key, (SECTIONS, TOKENS, KVHEADS, HEAD), jnp.float32), -4.0, 4.0)
    return (query_vals.reshape(SECTIONS, TOKENS, QW), key_vals.reshape(SECTIONS, TOKENS, KVW))


def draw_queries(key, part):
    return drawn_pair(key)[0].astype(jnp.bfloat16)


def draw_new_keys(key, part):
    return drawn_pair(key)[1].astype(jnp.bfloat16)


def levels(own_key, dims, cuts, least, largest):
    def one(dim, blocks):
        steps = jax.random.uniform(jax.random.fold_in(jax.random.fold_in(own_key, 6), dim), (blocks,), jnp.float32, least / len(cuts), largest / len(cuts))
        return jnp.repeat(jnp.exp(steps), dims[dim] // blocks).reshape((-1,) + (1,) * (len(dims) - dim - 1))

    loudness = one(*cuts[0])
    for cut in cuts[1:]:
        loudness = loudness * one(*cut)
    return loudness


def profile(number_of, total, limit, slope):
    weights = [(1 << 20) // math.isqrt(rank ** slope) + 1 for rank in range(2, number_of + 1)]
    surplus, given = total - limit - (number_of - 1), [1] * (number_of - 1)
    while surplus > 0:
        free = [i for i in range(number_of - 1) if given[i] < limit]
        pool, left = sum([weights[i] for i in free]), surplus
        for i in free:
            addition = min(limit - given[i], max(1, left * weights[i] // pool), surplus)
            given[i] = given[i] + addition
            surplus = surplus - addition
    return np.array([limit] + given)


def ragged(key, number_of, total, reach, skew):
    if number_of == 2:
        one = jax.random.randint(key, (), max(1, total - reach), min(reach, total - 1) + 1)
        return jnp.stack([one, total - one])
    sizes = jnp.asarray(profile(number_of, total, reach, skew), jnp.int32)
    pairs = (number_of - 1) // 2
    source_of, taker = sizes[1:1 + 2 * pairs:2], sizes[2:2 + 2 * pairs:2]
    margin = jnp.minimum(source_of - 1, reach - taker)
    shifted = jax.random.randint(jax.random.fold_in(key, 1), (pairs,), 0, 1 << 20) % (margin + 1)
    sizes = sizes.at[1:1 + 2 * pairs:2].set(source_of - shifted).at[2:2 + 2 * pairs:2].set(taker + shifted)
    return sizes[jax.random.permutation(jax.random.fold_in(key, 2), number_of)]


def gaussian(own_key, extent, spread, most, cuts=(), held_as=jnp.bfloat16):
    values = jax.random.normal(own_key, extent, jnp.float32) * spread
    if len(cuts) > 0:
        values = levels(own_key, extent, cuts, -0.22, 0.18) * values
    return jnp.clip(values, min=-most, max=most).astype(held_as)


def setup_inputs(seed: int = 0) -> dict:
    key_list = jax.random.split(jax.random.key(seed), 12)
    new_input = draw_new_input(jax.random.fold_in(key_list[11], 71), 0)
    new_gain = jnp.clip(1.0 + 0.1 * jax.random.normal(key_list[1], (SECTIONS, D), jnp.float32), 0.5, 1.5).astype(jnp.bfloat16)
    queries = draw_queries(jax.random.fold_in(key_list[11], 71), 0)
    new_keys = draw_new_keys(jax.random.fold_in(key_list[11], 71), 0)
    context_grad = gaussian(key_list[4], (SECTIONS, TOKENS, QW), 0.015, 0.08984375, ((0, 8), (1, 32)))
    segment_ids = jax.vmap(lambda own: jnp.searchsorted(jnp.cumsum(ragged(own, SEGS, TOKENS, TOK_DEV, 0)), jnp.arange(TOKENS), side="right"))(jax.random.split(key_list[5], SECTIONS)).reshape((SECTIONS, TOKENS)).astype(jnp.int32)
    frozen_input = draw_frozen_input(jax.random.fold_in(key_list[11], 71), 0)
    frozen_gain = jnp.clip(1.0 + 0.1 * jax.random.normal(key_list[7], (SECTIONS, D), jnp.float32), 0.5, 1.5).astype(jnp.bfloat16)
    output_grad = gaussian(key_list[8], (SECTIONS, TOKENS, D), 1.0, 6.0, ((0, 8), (1, 32)))
    kv_grad = gaussian(key_list[9], (SECTIONS, TOKENS, 2 * KVW), 3.0, 18.0, ((0, 8), (1, 32)))
    kv_weight = gaussian(key_list[10], (SECTIONS, D, 2 * KVW), D ** -0.5, 0.0625, ((0, 8), (1, 32)))
    return dict(new_input=new_input, new_gain=new_gain, queries=queries, new_keys=new_keys, context_grad=context_grad, segment_ids=segment_ids, frozen_input=frozen_input, frozen_gain=frozen_gain, output_grad=output_grad, kv_grad=kv_grad, kv_weight=kv_weight)


norm_eps = 1e-05
masked_value = -1e+30

def normalize(rows, gain):
    values = rows.astype(jnp.float32)
    inverse = lax.rsqrt(lax.optimization_barrier(jnp.mean(values * values, axis=-1, keepdims=True)) + norm_eps)
    return values * inverse * gain.astype(jnp.float32)

def norm_backward(rows, gain, upstream):
    values = rows.astype(jnp.float32)
    inverse = lax.rsqrt(lax.optimization_barrier(jnp.mean(values * values, axis=-1, keepdims=True)) + norm_eps)
    scaled = gain.astype(jnp.float32) * upstream
    inner_mean = lax.optimization_barrier(jnp.mean(values * scaled, axis=-1, keepdims=True))
    return inverse * scaled - values * inverse * inverse * inverse * inner_mean

def masked_softmax(scores, visible):
    masked = jnp.where(visible, scores, masked_value)
    highest = lax.optimization_barrier(jnp.max(masked, axis=-1, keepdims=True))
    weights = jnp.where(visible, jnp.exp(masked - highest), 0.0)
    return weights / lax.optimization_barrier(jnp.sum(weights, axis=-1, keepdims=True))

def one_sequence(members):
    query_rows, key_rows, grad_rows, seg_rows = members
    rows = query_rows.shape[0]
    query_four = query_rows.astype(jnp.float32).reshape(rows, KVHEADS, GROUP, HEAD)
    grad_four = grad_rows.astype(jnp.float32).reshape(rows, KVHEADS, GROUP, HEAD)
    key_three = key_rows.astype(jnp.float32).reshape(rows, KVHEADS, HEAD)
    position = jnp.arange(rows, dtype=jnp.int32)
    visible = (seg_rows[:, None] == seg_rows[None, :]) & (position[None, :] <= position[:, None])
    scores = jnp.einsum('tkgd,jkd->kgtj', query_four, key_three) / math.sqrt(HEAD)
    attention = masked_softmax(scores, visible).astype(jnp.bfloat16)
    return jnp.einsum('kgtj,tkgd->jkd', attention.astype(jnp.float32), grad_four).reshape(rows, KVW)

def attend_values(query_rows, key_rows, grad_rows, seg_rows):
    count = query_rows.shape[0] // TOK_DEV
    members = (query_rows.reshape(count, TOK_DEV, QW), key_rows.reshape(count, TOK_DEV, KVW), grad_rows.reshape(count, TOK_DEV, QW), seg_rows.astype(jnp.int32).reshape(count, TOK_DEV))
    return lax.map(one_sequence, members).reshape(count * TOK_DEV, KVW)

def reference(new_input, new_gain, queries, new_keys, context_grad, segment_ids, frozen_input, frozen_gain, output_grad, kv_grad, kv_weight):
    grad_list = []
    cot_list = []
    for section_at in range(SECTIONS):
        normed_new = normalize(new_input[section_at], new_gain[section_at]).astype(jnp.bfloat16)
        value_cot = attend_values(queries[section_at], new_keys[section_at], context_grad[section_at], segment_ids[section_at]).astype(jnp.bfloat16)
        grad_list.append(jnp.dot(normed_new.T, value_cot, preferred_element_type=jnp.float32))
        normed_cot = jnp.dot(kv_grad[section_at], kv_weight[section_at].T, preferred_element_type=jnp.float32).astype(jnp.bfloat16)
        normed_cot = lax.optimization_barrier(normed_cot)
        input_cot = output_grad[section_at].astype(jnp.float32) + norm_backward(frozen_input[section_at], frozen_gain[section_at], normed_cot.astype(jnp.float32))
        cot_list.append(input_cot.astype(jnp.bfloat16))
    cot_below = jnp.stack(cot_list[1:] + [jnp.zeros_like(cot_list[0])], axis=0)
    return (cot_below, jnp.stack(grad_list, axis=0))
```

```python
import functools
import math

import jax
import jax.numpy as jnp
from jax import lax
from jax.experimental import pallas as pl
from jax.experimental.pallas import tpu as pltpu
from jax.sharding import PartitionSpec as P

HEAD = 128
NORM_EPS = 1e-05
MASKED = -1e30

MESH = pl.DeviceIdType.MESH
F32 = jnp.float32
BF16 = jnp.bfloat16

RING = 8
TEAM = 4
ROWS = 128
WIDTH = 8192
CHUNK = 256
CHUNKS = 32
QUARTER = 2048
VW = 512
KW = 1024
PARTS = 4
SUBS = 2
SUBROWS = 128 // SUBS
PIECES = 8
PIECE = WIDTH // PIECES


def kernel(
    sections,
    x_new, g_new, q_in, k_in, ctx_in, seg_in, x_frz, g_frz, og_in, kv_in, w_in,
    cot_out, vg_out,
    xn, gn, qv, kk, cx, sg, xf, gf, og, kvt, wbuf, rst, nc, nst, nt, vst, vt,
    pblk, rs_send, rs_recv, ost, vgb, s2, sq,
    load_sem, kv_ssem, kv_rsem, w_ssem, w_rsem, r_ssem, nc_rsem, n_ssem, n_rsem,
    v_ssem, v_rsem, rs_ssem, rs_rsem, c_ssem, c_rsem, own_sem, out_sem,
):
    p = lax.axis_index("pipe")
    d = lax.axis_index("dp")
    y = d // 16
    z = (d // 2) % RING
    c = d % 2
    q = y * 2 + c

    def at(yy, zz, cc):
        return yy * 16 + zz * 2 + cc

    right = at(y, (z + 1) % RING, c)
    left = at(y, (z + RING - 1) % RING, c)
    core_mate = at(y, z, 1 - c)
    chip_mate = at(1 - y, z, c)
    cross_mate = at(1 - y, z, 1 - c)

    def remote(src, dst, ssem, rsem, dev):
        return pltpu.make_async_remote_copy(
            src_ref=src, dst_ref=dst, send_sem=ssem, recv_sem=rsem,
            device_id={"dp": dev}, device_id_type=MESH)

    def below(src, dst, ssem, rsem):
        return pltpu.make_async_remote_copy(
            src_ref=src, dst_ref=dst, send_sem=ssem, recv_sem=rsem,
            device_id={"pipe": lax.rem(p + sections - 1, sections)}, device_id_type=MESH)

    loads = [
        pltpu.make_async_copy(x_new, xn, load_sem.at[0]),
        pltpu.make_async_copy(g_new, gn, load_sem.at[1]),
        pltpu.make_async_copy(seg_in, sg, load_sem.at[2]),
        pltpu.make_async_copy(k_in, kk, load_sem.at[3]),
        pltpu.make_async_copy(q_in, qv, load_sem.at[4]),
        pltpu.make_async_copy(ctx_in, cx, load_sem.at[5]),
        pltpu.make_async_copy(kv_in, kvt.at[q], load_sem.at[6]),
        pltpu.make_async_copy(w_in, wbuf.at[z], load_sem.at[7]),
        pltpu.make_async_copy(x_frz, xf, load_sem.at[8]),
        pltpu.make_async_copy(g_frz, gf, load_sem.at[9]),
        pltpu.make_async_copy(og_in, og, load_sem.at[10]),
    ]
    for load in loads:
        load.start()

    barrier = pltpu.get_barrier_semaphore()
    for dev in (right, left, core_mate, chip_mate, cross_mate):
        pl.semaphore_signal(barrier, inc=1, device_id={"dp": dev}, device_id_type=MESH)

    @pl.when(p > 0)
    def _():
        pl.semaphore_signal(barrier, inc=1, device_id={"pipe": lax.rem(p + sections - 1, sections)}, device_id_type=MESH)

    @pl.when(p < sections - 1)
    def _():
        pl.semaphore_signal(barrier, inc=1, device_id={"pipe": lax.rem(p + 1, sections)}, device_id_type=MESH)

    pl.semaphore_wait(barrier, 5 + jnp.where(p > 0, 1, 0) + jnp.where(p < sections - 1, 1, 0))

    def half(slot, h):
        return wbuf.at[slot, pl.ds(h * 128, 128)]

    def zz(k):
        return (z + RING + k) % RING

    def w_copy(way, k, h, own=False):
        slot = zz(-k) if way == 0 else zz(k)
        n = 2 * k + (h if k < 3 else 0)
        src = w_in.at[pl.ds(h * 128, 128)] if own else half(slot, h)
        return remote(src, half(slot, h), w_ssem.at[way, n], w_rsem.at[way, n], right if way == 0 else left)

    def w_arrival(way, k, h):
        slot = zz(-(k + 1)) if way == 0 else zz(k + 1)
        n = 2 * k + (h if k < 3 else 0)
        return remote(half(slot, h), half(slot, h), w_ssem.at[way, n], w_rsem.at[way, n], right if way == 0 else left)

    sent = []

    def start(copy):
        copy.start()
        sent.append(copy)

    for h in range(2):
        start(w_copy(0, 0, h, own=True))
        start(w_copy(1, 0, h, own=True))

    start(remote(kv_in, kvt.at[q], kv_ssem.at[0], kv_rsem.at[0], chip_mate))
    start(remote(kv_in, kvt.at[q], kv_ssem.at[1], kv_rsem.at[1], core_mate))

    q_core = y * 2 + (1 - c)
    q_chip = (1 - y) * 2 + c
    q_cross = (1 - y) * 2 + (1 - c)

    loads[0].wait()
    loads[1].wait()
    sq[...] = jnp.zeros_like(sq)

    @pl.loop(0, CHUNKS)
    def _(j):
        v = xn[:, pl.ds(pl.multiple_of(j * CHUNK, CHUNK), CHUNK)].astype(F32)
        v = v * v
        sq[...] += v[:, :128] + v[:, 128:]

    inv_new = lax.rsqrt(jnp.sum(sq[...], axis=1, keepdims=True) / WIDTH + NORM_EPS)

    @pl.loop(0, CHUNKS)
    def _(j):
        cols = pl.ds(pl.multiple_of(j * CHUNK, CHUNK), CHUNK)
        v = xn[:, cols].astype(F32) * inv_new * gn[:, cols].astype(F32)
        role = (j // 16) * 2 + j % 2
        nst[role, :, pl.ds(pl.multiple_of(((j // 2) % RING) * CHUNK, CHUNK), CHUNK)] = v.astype(BF16)

    def n_copy(index, role, dev, part):
        cols = pl.ds(part * (QUARTER // PARTS), QUARTER // PARTS)
        return remote(nst.at[role, :, cols], nt.at[q, :, cols], n_ssem.at[index, part], n_rsem.at[index, part], dev)

    def n_part(part):
        start(n_copy(1, q_chip, chip_mate, part))
        start(n_copy(2, q_cross, cross_mate, part))

    own_n = pltpu.make_async_copy(nst.at[q], nt.at[q], own_sem.at[0])
    own_n.start()
    n_part(0)
    for part in range(PARTS):
        start(n_copy(0, q_core, core_mate, part))

    def forward(way, k, h):
        w_arrival(way, k, h).wait_recv()
        start(w_copy(way, k + 1, h))

    forward(0, 0, 0)
    forward(1, 0, 0)

    remote(kv_in, kvt.at[q_chip], kv_ssem.at[0], kv_rsem.at[0], chip_mate).wait_recv()
    start(remote(kvt.at[q_chip], kvt.at[q_chip], kv_ssem.at[2], kv_rsem.at[2], core_mate))

    n_part(1)

    for load in loads[2:6]:
        load.wait()
    seg_i = jnp.broadcast_to(sg[...].astype(F32), (ROWS, ROWS))
    seg_j = seg_i.T
    pos_j = lax.broadcasted_iota(jnp.int32, (ROWS, ROWS), 0)
    pos_i = lax.broadcasted_iota(jnp.int32, (ROWS, ROWS), 1)
    visible_one = jnp.where((seg_i == seg_j) & (pos_j <= pos_i), 1.0, 0.0)
    scale = 1.0 / math.sqrt(HEAD)

    @pl.loop(0, 4)
    def _(g):
        keys = kk[:, pl.ds(pl.multiple_of(g * HEAD, HEAD), HEAD)]
        total = jnp.zeros((ROWS, HEAD), F32)
        for h in range(8):
            cols = pl.ds(pl.multiple_of(g * 8 * HEAD + h * HEAD, HEAD), HEAD)
            s = lax.dot_general(keys, qv[:, cols], (((1,), (1,)), ((), ())), preferred_element_type=F32) * scale
            seen = visible_one > 0.5
            s = jnp.where(seen, s, MASKED)
            top = jnp.max(s, axis=0, keepdims=True)
            e = jnp.where(seen, jnp.exp(s - top), 0.0)
            a = (e / jnp.sum(e, axis=0, keepdims=True)).astype(BF16)
            total += jnp.dot(a, cx[:, cols], preferred_element_type=F32)
        vst[:, pl.ds(pl.multiple_of(g * HEAD, HEAD), HEAD)] = total.astype(BF16)

    start(remote(vst, vt.at[q], v_ssem.at[0], v_rsem.at[0], chip_mate))
    start(remote(vst, vt.at[q], v_ssem.at[1], v_rsem.at[1], core_mate))
    own_v = pltpu.make_async_copy(vst, vt.at[q], own_sem.at[1])
    own_v.start()

    forward(0, 0, 1)
    forward(1, 0, 1)

    for load in loads[6:11]:
        load.wait()
    remote(kv_in, kvt.at[q_core], kv_ssem.at[1], kv_rsem.at[1], core_mate).wait_recv()
    remote(kv_in, kvt.at[q_cross], kv_ssem.at[2], kv_rsem.at[2], core_mate).wait_recv()

    s2[...] = jnp.zeros_like(s2)

    def accumulate(j):
        cols = pl.ds(pl.multiple_of(j * CHUNK, CHUNK), CHUNK)
        v = xf[:, cols].astype(F32) * (gf[:, cols].astype(F32) * nc[j].astype(F32))
        s2[...] += v[:, :128] + v[:, 128:]

    def result_copy(slot, index, role, dev):
        j = at(y, slot, c)
        return remote(rst.at[slot, role], nc.at[j], r_ssem.at[slot, index], nc_rsem.at[index, slot], dev)

    def multiply(slot):
        w = wbuf[slot]
        for m in range(2):
            kv = kvt[pl.ds(2 * m, 2)].reshape(2 * ROWS, KW)
            r = lax.dot_general(kv, w, (((1,), (1,)), ((), ())), preferred_element_type=F32)
            rst[slot, pl.ds(2 * m, 2)] = r.astype(BF16).reshape(2, ROWS, CHUNK)
        start(result_copy(slot, 1, q_chip, chip_mate))
        start(result_copy(slot, 2, q_cross, cross_mate))
        start(result_copy(slot, 0, q_core, core_mate))
        nc[at(y, slot, c)] = rst[slot, q]
        accumulate(at(y, slot, c))

    def gather(slot):
        for index, (yy, cc) in ((0, (y, 1 - c)), (1, (1 - y, c)), (2, (1 - y, 1 - c))):
            j = at(yy, slot, cc)
            remote(rst.at[slot, 0], nc.at[j], r_ssem.at[slot, index], nc_rsem.at[index, slot], chip_mate).wait_recv()
            accumulate(j)

    multiply(z)
    multiply(zz(-1))
    multiply(zz(1))

    remote(vst, vt.at[q_chip], v_ssem.at[0], v_rsem.at[0], chip_mate).wait_recv()
    start(remote(vt.at[q_chip], vt.at[q_chip], v_ssem.at[2], v_rsem.at[2], core_mate))

    forward(0, 1, 0)
    forward(1, 1, 0)

    sq[...] = jnp.zeros_like(sq)

    @pl.loop(0, CHUNKS)
    def _(j):
        v = xf[:, pl.ds(pl.multiple_of(j * CHUNK, CHUNK), CHUNK)].astype(F32)
        v = v * v
        sq[...] += v[:, :128] + v[:, 128:]

    gather(z)

    forward(0, 1, 1)
    forward(1, 1, 1)
    multiply(zz(-2))
    multiply(zz(2))
    n_part(2)
    gather(zz(-1))
    gather(zz(1))

    forward(0, 2, 0)
    w_arrival(1, 2, 0).wait_recv()
    gather(zz(-2))
    gather(zz(2))
    forward(1, 2, 1)
    w_arrival(0, 2, 1).wait_recv()
    multiply(zz(-3))
    multiply(zz(3))
    gather(zz(-3))
    gather(zz(3))
    w_arrival(0, 3, 0).wait_recv()
    w_arrival(1, 3, 1).wait_recv()
    multiply(zz(4))
    n_part(3)
    gather(zz(4))

    inv = lax.rsqrt(jnp.sum(sq[...], axis=1, keepdims=True) / WIDTH + NORM_EPS)
    mean = jnp.sum(s2[...], axis=1, keepdims=True) / WIDTH
    back = inv * inv * inv * mean

    def piece_copy(i):
        cols = pl.ds(i * PIECE, PIECE)
        return below(ost.at[:, cols], cot_out.at[:, cols], c_ssem.at[i], c_rsem.at[i])

    for i in range(PIECES):
        @pl.loop(0, PIECE // CHUNK)
        def _(k):
            j = i * (PIECE // CHUNK) + k
            cols = pl.ds(pl.multiple_of(j * CHUNK, CHUNK), CHUNK)
            scaled = gf[:, cols].astype(F32) * nc[j].astype(F32)
            v = og[:, cols].astype(F32) + inv * scaled - xf[:, cols].astype(F32) * back
            ost[:, cols] = v.astype(BF16)

        @pl.when(p > 0)
        def _():
            piece_copy(i).start()

    own_n.wait()
    own_v.wait()
    remote(vst, vt.at[q_core], v_ssem.at[1], v_rsem.at[1], core_mate).wait_recv()
    remote(vst, vt.at[q_cross], v_ssem.at[2], v_rsem.at[2], core_mate).wait_recv()
    for index, role in ((0, q_core), (1, q_chip), (2, q_cross)):
        for part in range(PARTS):
            cols = pl.ds(part * (QUARTER // PARTS), QUARTER // PARTS)
            remote(nst.at[0, :, cols], nt.at[role, :, cols], n_ssem.at[index, part], n_rsem.at[index, part], core_mate).wait_recv()

    @pl.loop(0, RING)
    def _(b):
        left_side = nt[:, :, pl.ds(pl.multiple_of(b * CHUNK, CHUNK), CHUNK)].reshape(TEAM * ROWS, CHUNK)
        pblk[b] = lax.dot_general(left_side, vt[...].reshape(TEAM * ROWS, VW), (((0,), (0,)), ((), ())), preferred_element_type=F32)

    def rs_copy(way, sub, s):
        return remote(rs_send.at[way, s, sub], rs_recv.at[way, s, sub], rs_ssem.at[way, s, sub], rs_rsem.at[way, s, sub], right if way == 0 else left)

    for s in range(RING - 1):
        for sub in range(SUBS):
            for way in range(2):
                b = zz(-1 - s) if way == 0 else zz(1 + s)
                rows = pl.ds(way * 128 + sub * SUBROWS, SUBROWS)
                v = pblk[b, rows]
                if s > 0:
                    rs_copy(way, sub, s - 1).wait_recv()
                    v += rs_recv[way, s - 1, sub].astype(F32)
                rs_send[way, s, sub] = v.astype(BF16)
                start(rs_copy(way, sub, s))
    outs = []
    for sub in range(SUBS):
        for way in range(2):
            rows = pl.ds(way * 128 + sub * SUBROWS, SUBROWS)
            rs_copy(way, sub, RING - 2).wait_recv()
            vgb[rows] = pblk[z, rows] + rs_recv[way, RING - 2, sub].astype(F32)
    vg_copy = pltpu.make_async_copy(vgb, vg_out, out_sem.at[0])
    vg_copy.start()

    @pl.when(p == sections - 1)
    def _():
        ones = []
        for i in range(PIECES):
            piece_copy(i).wait_send()
        ost[...] = jnp.zeros_like(ost)
        zero = pltpu.make_async_copy(ost, cot_out, out_sem.at[1])
        zero.start()
        zero.wait()

    @pl.when((p > 0) & (p < sections - 1))
    def _():
        for i in range(PIECES):
            piece_copy(i).wait_send()

    @pl.when(p < sections - 1)
    def _():
        for i in range(PIECES):
            piece_copy(i).wait_recv()

    vg_copy.wait()
    for copy in sent:
        copy.wait_send()


def shards(sections, *args):
    args = [a[0] if a.ndim == 3 else a for a in args]
    any_space = pl.BlockSpec(memory_space=pl.ANY)
    dma = pltpu.SemaphoreType.DMA
    cot, vg = pl.pallas_call(
        functools.partial(kernel, sections),
        out_shape=(
            jax.ShapeDtypeStruct((ROWS, WIDTH), BF16),
            jax.ShapeDtypeStruct((CHUNK, VW), F32),
        ),
        in_specs=[any_space] * 11,
        out_specs=(any_space, any_space),
        scratch_shapes=[
            pltpu.VMEM((ROWS, WIDTH), BF16),
            pltpu.VMEM((1, WIDTH), BF16),
            pltpu.VMEM((ROWS, 4096), BF16),
            pltpu.VMEM((ROWS, VW), BF16),
            pltpu.VMEM((ROWS, 4096), BF16),
            pltpu.VMEM((1, ROWS), jnp.int32),
            pltpu.VMEM((ROWS, WIDTH), BF16),
            pltpu.VMEM((1, WIDTH), BF16),
            pltpu.VMEM((ROWS, WIDTH), BF16),
            pltpu.VMEM((TEAM, ROWS, KW), BF16),
            pltpu.VMEM((RING, CHUNK, KW), BF16),
            pltpu.VMEM((RING, TEAM, ROWS, CHUNK), BF16),
            pltpu.VMEM((CHUNKS, ROWS, CHUNK), BF16),
            pltpu.VMEM((TEAM, ROWS, QUARTER), BF16),
            pltpu.VMEM((TEAM, ROWS, QUARTER), BF16),
            pltpu.VMEM((ROWS, VW), BF16),
            pltpu.VMEM((TEAM, ROWS, VW), BF16),
            pltpu.VMEM((RING, CHUNK, VW), F32),
            pltpu.VMEM((2, RING - 1, SUBS, SUBROWS, VW), BF16),
            pltpu.VMEM((2, RING - 1, SUBS, SUBROWS, VW), BF16),
            pltpu.VMEM((ROWS, WIDTH), BF16),
            pltpu.VMEM((CHUNK, VW), F32),
            pltpu.VMEM((ROWS, 128), F32),
            pltpu.VMEM((ROWS, 128), F32),
            dma((11,)),
            dma((3,)), dma((3,)),
            dma((2, 7)), dma((2, 7)),
            dma((RING, 3)), dma((3, RING)),
            dma((3, PARTS)), dma((3, PARTS)),
            dma((3,)), dma((3,)),
            dma((2, RING - 1, SUBS)), dma((2, RING - 1, SUBS)),
            dma((PIECES,)), dma((PIECES,)),
            dma((2,)), dma((2,)),
        ],
        compiler_params=pltpu.CompilerParams(
            collective_id=0, has_side_effects=True, vmem_limit_bytes=60 * 1024 * 1024),
        cost_estimate=pl.CostEstimate(flops=6_000_000_000, bytes_accessed=20_000_000, transcendentals=600_000),
    )(*args)
    return cot[None], vg[None]


def solution(mesh):
    placed = (
        P("pipe", "dp", None),
        P("pipe", None),
        P("pipe", "dp", None),
        P("pipe", "dp", None),
        P("pipe", "dp", None),
        P("pipe", "dp"),
        P("pipe", "dp", None),
        P("pipe", None),
        P("pipe", "dp", None),
        P("pipe", "dp", None),
        P("pipe", "dp", None),
    )
    return jax.shard_map(
        functools.partial(shards, mesh.shape["pipe"]),
        mesh=mesh,
        in_specs=placed,
        out_specs=(P("pipe", "dp", None), P("pipe", "dp", None)),
        check_vma=False,
    )
```

```python
import functools
import math

import jax
import jax.numpy as jnp
from jax import lax
from jax.experimental import pallas as pl
from jax.experimental.pallas import tpu as pltpu
from jax.sharding import PartitionSpec as P

HEAD = 128
NORM_EPS = 1e-05
MASKED = -1e30

MESH = pl.DeviceIdType.MESH
F32 = jnp.float32
BF16 = jnp.bfloat16

RING = 8
TEAM = 4
ROWS = 128
WIDTH = 8192
CHUNK = 256
CHUNKS = 32
QUARTER = 2048
VW = 512
KW = 1024
PARTS = 4
SUBS = 4
SUBROWS = 128 // SUBS
OFFSETS = (0, -1, 1, -2, 2, -3, 3, 4)
EARLY = 4


def kernel(
    sections,
    x_new, g_new, q_in, k_in, ctx_in, seg_in, x_frz, g_frz, og_in, kv_in, w_in,
    cot_out, vg_out,
    xn, gn, qv, kk, cx, sg, xf, gf, og, kvt, wbuf, rst, nc, nst, nt, vst, vt,
    pblk, rs_send, rs_recv, fin, ast, ar, xr, relay, back_send, back_recv, invb, s2, sq,
    load_sem, kv_ssem, kv_rsem, w_ssem, w_rsem, r_ssem, nc_rsem, n_ssem, n_rsem,
    v_ssem, v_rsem, rs_ssem, rs_rsem, c_ssem, c_rsem, x_ssem, x_rsem, a_ssem, a_rsem,
    b_ssem, b_rsem, rl_ssem, rl_rsem, own_sem,
):
    p = lax.axis_index("pipe")
    d = lax.axis_index("dp")
    y = d // 16
    z = (d // 2) % RING
    c = d % 2
    q = y * 2 + c

    def at(yy, zz, cc):
        return yy * 16 + zz * 2 + cc

    right = at(y, (z + 1) % RING, c)
    left = at(y, (z + RING - 1) % RING, c)
    core_mate = at(y, z, 1 - c)
    chip_mate = at(1 - y, z, c)
    cross_mate = at(1 - y, z, 1 - c)

    def remote(src, dst, ssem, rsem, dev):
        return pltpu.make_async_remote_copy(
            src_ref=src, dst_ref=dst, send_sem=ssem, recv_sem=rsem,
            device_id={"dp": dev}, device_id_type=MESH)

    mid = sections // 2
    below_p = lax.rem(p + sections - 1, sections)
    early_sender = (p > 0) & (p != mid)
    early_receiver = (p < sections - 1) & (p != mid - 1)

    def to(src, dst, ssem, rsem, pipe, dev):
        return pltpu.make_async_remote_copy(
            src_ref=src, dst_ref=dst, send_sem=ssem, recv_sem=rsem,
            device_id={"pipe": pipe, "dp": dev}, device_id_type=MESH)

    def signal(pipe, dev):
        pl.semaphore_signal(barrier, inc=1, device_id={"pipe": pipe, "dp": dev}, device_id_type=MESH)

    loads = [
        pltpu.make_async_copy(x_new, xn, load_sem.at[0]),
        pltpu.make_async_copy(g_new, gn, load_sem.at[1]),
        pltpu.make_async_copy(seg_in, sg, load_sem.at[2]),
        pltpu.make_async_copy(k_in, kk, load_sem.at[3]),
        pltpu.make_async_copy(q_in, qv, load_sem.at[4]),
        pltpu.make_async_copy(ctx_in, cx, load_sem.at[5]),
        pltpu.make_async_copy(kv_in, kvt.at[q], load_sem.at[6]),
        pltpu.make_async_copy(w_in, wbuf.at[z], load_sem.at[7]),
        pltpu.make_async_copy(x_frz, xf, load_sem.at[8]),
        pltpu.make_async_copy(g_frz, gf, load_sem.at[9]),
        pltpu.make_async_copy(og_in, og, load_sem.at[10]),
    ]
    for load in loads:
        load.start()

    barrier = pltpu.get_barrier_semaphore()
    for dev in (right, left, core_mate, chip_mate, cross_mate):
        pl.semaphore_signal(barrier, inc=1, device_id={"dp": dev}, device_id_type=MESH)

    @pl.when(p > 0)
    def _():
        signal(below_p, d)

    @pl.when(p < sections - 1)
    def _():
        signal(lax.rem(p + 1, sections), d)

    @pl.when(p == mid)
    def _():
        signal(0, chip_mate)

    @pl.when(p == 0)
    def _():
        signal(mid, chip_mate)
        signal(mid - 1, chip_mate)

    @pl.when(p == mid - 1)
    def _():
        signal(0, chip_mate)

    pl.semaphore_wait(
        barrier,
        5 + jnp.where(p > 0, 1, 2) + jnp.where(p < sections - 1, 1, 0)
        + jnp.where((p == mid) | (p == mid - 1), 1, 0))

    def half(slot, h):
        return wbuf.at[slot, pl.ds(h * 128, 128)]

    def zz(k):
        return (z + RING + k) % RING

    def w_copy(way, k, h, own=False):
        slot = zz(-k) if way == 0 else zz(k)
        n = 2 * k + (h if k < 3 else 0)
        src = w_in.at[pl.ds(h * 128, 128)] if own else half(slot, h)
        return remote(src, half(slot, h), w_ssem.at[way, n], w_rsem.at[way, n], right if way == 0 else left)

    def w_arrival(way, k, h):
        slot = zz(-(k + 1)) if way == 0 else zz(k + 1)
        n = 2 * k + (h if k < 3 else 0)
        return remote(half(slot, h), half(slot, h), w_ssem.at[way, n], w_rsem.at[way, n], right if way == 0 else left)

    sent = []

    def start(copy):
        copy.start()
        sent.append(copy)

    for h in range(2):
        start(w_copy(0, 0, h, own=True))
        start(w_copy(1, 0, h, own=True))

    start(remote(kv_in, kvt.at[q], kv_ssem.at[0], kv_rsem.at[0], chip_mate))
    start(remote(kv_in, kvt.at[q], kv_ssem.at[1], kv_rsem.at[1], core_mate))

    def chunk_cols(j):
        return pl.ds(pl.multiple_of(j * CHUNK, CHUNK), CHUNK)

    def x_copy(i, yy):
        cols = pl.ds(pl.multiple_of(at(yy, zz(OFFSETS[i]), 0) * CHUNK, 2 * CHUNK), 2 * CHUNK)
        return to(x_frz.at[:, cols], xr.at[i * 2 + yy], x_ssem.at[i * 2 + yy], x_rsem.at[i * 2 + yy], below_p, d)

    @pl.when(early_sender)
    def _():
        for i in range(EARLY):
            for yy in range(2):
                x_copy(i, yy).start()

    q_core = y * 2 + (1 - c)
    q_chip = (1 - y) * 2 + c
    q_cross = (1 - y) * 2 + (1 - c)

    loads[0].wait()
    loads[1].wait()
    sq[...] = jnp.zeros_like(sq)

    @pl.loop(0, CHUNKS)
    def _(j):
        v = xn[:, pl.ds(pl.multiple_of(j * CHUNK, CHUNK), CHUNK)].astype(F32)
        v = v * v
        sq[...] += v[:, :128] + v[:, 128:]

    inv_new = lax.rsqrt(jnp.sum(sq[...], axis=1, keepdims=True) / WIDTH + NORM_EPS)

    @pl.loop(0, CHUNKS)
    def _(j):
        cols = pl.ds(pl.multiple_of(j * CHUNK, CHUNK), CHUNK)
        v = xn[:, cols].astype(F32) * inv_new * gn[:, cols].astype(F32)
        role = (j // 16) * 2 + j % 2
        block = ((j // 2) % RING) * 128
        v = v.astype(BF16)
        nst[role, :, pl.ds(pl.multiple_of(block, 128), 128)] = v[:, :128]
        nst[role, :, pl.ds(pl.multiple_of(block + RING * 128, 128), 128)] = v[:, 128:]

    def n_copy(index, role, dev, part):
        cols = pl.ds(part * (QUARTER // PARTS), QUARTER // PARTS)
        return remote(nst.at[role, :, cols], nt.at[q, :, cols], n_ssem.at[index, part], n_rsem.at[index, part], dev)

    def n_part(part):
        start(n_copy(1, q_chip, chip_mate, part))
        start(n_copy(2, q_cross, cross_mate, part))

    own_n = pltpu.make_async_copy(nst.at[q], nt.at[q], own_sem.at[0])
    own_n.start()
    n_part(0)
    for part in range(PARTS):
        start(n_copy(0, q_core, core_mate, part))

    def forward(way, k, h):
        w_arrival(way, k, h).wait_recv()
        start(w_copy(way, k + 1, h))

    n_part(1)

    forward(0, 0, 0)
    forward(1, 0, 0)

    remote(kv_in, kvt.at[q_chip], kv_ssem.at[0], kv_rsem.at[0], chip_mate).wait_recv()
    start(remote(kvt.at[q_chip], kvt.at[q_chip], kv_ssem.at[2], kv_rsem.at[2], core_mate))

    for load in loads[2:6]:
        load.wait()
    seg_i = jnp.broadcast_to(sg[...].astype(F32), (ROWS, ROWS))
    seg_j = seg_i.T
    pos_j = lax.broadcasted_iota(jnp.int32, (ROWS, ROWS), 0)
    pos_i = lax.broadcasted_iota(jnp.int32, (ROWS, ROWS), 1)
    visible_one = jnp.where((seg_i == seg_j) & (pos_j <= pos_i), 1.0, 0.0)
    scale = 1.0 / math.sqrt(HEAD)

    @pl.loop(0, 4)
    def _(g):
        keys = kk[:, pl.ds(pl.multiple_of(g * HEAD, HEAD), HEAD)]
        total = jnp.zeros((ROWS, HEAD), F32)
        for h in range(8):
            cols = pl.ds(pl.multiple_of(g * 8 * HEAD + h * HEAD, HEAD), HEAD)
            s = lax.dot_general(keys, qv[:, cols], (((1,), (1,)), ((), ())), preferred_element_type=F32) * scale
            seen = visible_one > 0.5
            s = jnp.where(seen, s, MASKED)
            top = jnp.max(s, axis=0, keepdims=True)
            e = jnp.where(seen, jnp.exp(s - top), 0.0)
            a = (e / jnp.sum(e, axis=0, keepdims=True)).astype(BF16)
            total += jnp.dot(a, cx[:, cols], preferred_element_type=F32)
        vst[:, pl.ds(pl.multiple_of(g * HEAD, HEAD), HEAD)] = total.astype(BF16)

    start(remote(vst, vt.at[q], v_ssem.at[0], v_rsem.at[0], chip_mate))
    start(remote(vst, vt.at[q], v_ssem.at[1], v_rsem.at[1], core_mate))
    own_v = pltpu.make_async_copy(vst, vt.at[q], own_sem.at[1])
    own_v.start()

    forward(0, 0, 1)
    forward(1, 0, 1)

    for load in loads[6:11]:
        load.wait()
    remote(kv_in, kvt.at[q_core], kv_ssem.at[1], kv_rsem.at[1], core_mate).wait_recv()
    remote(kv_in, kvt.at[q_cross], kv_ssem.at[2], kv_rsem.at[2], core_mate).wait_recv()

    s2[...] = jnp.zeros_like(s2)
    sq[...] = jnp.zeros_like(sq)

    @pl.loop(0, CHUNKS)
    def _(j):
        v = xf[:, chunk_cols(j)].astype(F32)
        v = v * v
        sq[...] += v[:, :128] + v[:, 128:]

    inv_frz = lax.rsqrt(jnp.sum(sq[...], axis=1, keepdims=True) / WIDTH + NORM_EPS)
    invb[...] = jnp.broadcast_to(inv_frz, (ROWS, 128))

    def twice(ref):
        v = ref[...]
        return jnp.concatenate([v, v], axis=1)

    def a_copy(slot):
        return to(ast.at[slot], ar.at[slot], a_ssem.at[slot], a_rsem.at[slot], below_p, d)

    def accumulate(i, yy, cc):
        j = at(yy, zz(OFFSETS[i]), cc)
        cols = chunk_cols(j)
        scaled = gf[:, cols].astype(F32) * nc[j].astype(F32)
        v = xf[:, cols].astype(F32) * scaled
        s2[...] += v[:, :128] + v[:, 128:]
        if i < EARLY:
            slot = i * 4 + yy * 2 + cc
            ast[slot] = (og[:, cols].astype(F32) + twice(invb) * scaled).astype(BF16)

            @pl.when(early_sender)
            def _():
                a_copy(slot).start()

    def result_copy(slot, index, role, dev):
        j = at(y, slot, c)
        return remote(rst.at[slot, role], nc.at[j], r_ssem.at[slot, index], nc_rsem.at[index, slot], dev)

    def multiply(i):
        slot = zz(OFFSETS[i])
        w = wbuf[slot]
        for m in range(2):
            kv = kvt[pl.ds(2 * m, 2)].reshape(2 * ROWS, KW)
            r = lax.dot_general(kv, w, (((1,), (1,)), ((), ())), preferred_element_type=F32)
            rst[slot, pl.ds(2 * m, 2)] = r.astype(BF16).reshape(2, ROWS, CHUNK)
        start(result_copy(slot, 1, q_chip, chip_mate))
        start(result_copy(slot, 2, q_cross, cross_mate))
        start(result_copy(slot, 0, q_core, core_mate))
        nc[at(y, slot, c)] = rst[slot, q]
        accumulate(i, y, c)

    def gather(i):
        slot = zz(OFFSETS[i])
        for index, (yy, cc) in ((0, (y, 1 - c)), (1, (1 - y, c)), (2, (1 - y, 1 - c))):
            j = at(yy, slot, cc)
            remote(rst.at[slot, 0], nc.at[j], r_ssem.at[slot, index], nc_rsem.at[index, slot], chip_mate).wait_recv()
            accumulate(i, yy, cc)

    def partial_sums(way):
        for index, role in ((0, q_core), (1, q_chip), (2, q_cross)):
            for part in (2 * way, 2 * way + 1):
                cols = pl.ds(part * (QUARTER // PARTS), QUARTER // PARTS)
                remote(nst.at[0, :, cols], nt.at[role, :, cols], n_ssem.at[index, part], n_rsem.at[index, part], core_mate).wait_recv()

        @pl.loop(0, RING // 2)
        def _(i):
            cols = pl.ds(pl.multiple_of(way * RING * 128 + i * 256, 256), 256)
            rows = nt[:, :, cols].reshape(TEAM * ROWS, 256)
            r = lax.dot_general(rows, vt[...].reshape(TEAM * ROWS, VW), (((0,), (0,)), ((), ())), preferred_element_type=F32)
            pblk[way, pl.ds(2 * i, 2)] = r.reshape(2, 128, VW)

    def rs_copy(way, sub, s):
        return remote(rs_send.at[way, s, sub], rs_recv.at[way, s, sub], rs_ssem.at[way, s, sub], rs_rsem.at[way, s, sub], right if way == 0 else left)

    def rs_step(way, s):
        b = zz(-1 - s) if way == 0 else zz(1 + s)
        for sub in range(SUBS):
            v = pblk[way, b, pl.ds(sub * SUBROWS, SUBROWS)]
            if s > 0:
                rs_copy(way, sub, s - 1).wait_recv()
                v += rs_recv[way, s - 1, sub].astype(F32)
            rs_send[way, s, sub] = v.astype(BF16)
            start(rs_copy(way, sub, s))

    def rs_end(way):
        for sub in range(SUBS):
            rs_copy(way, sub, RING - 2).wait_recv()
            vg_out[pl.ds(way * 128 + sub * SUBROWS, SUBROWS)] = (
                pblk[way, z, pl.ds(sub * SUBROWS, SUBROWS)] + rs_recv[way, RING - 2, sub].astype(F32))

    multiply(0)
    multiply(1)
    multiply(2)
    n_part(2)

    remote(vst, vt.at[q_chip], v_ssem.at[0], v_rsem.at[0], chip_mate).wait_recv()
    start(remote(vt.at[q_chip], vt.at[q_chip], v_ssem.at[2], v_rsem.at[2], core_mate))

    forward(0, 1, 0)
    forward(1, 1, 0)
    gather(0)
    forward(0, 1, 1)
    forward(1, 1, 1)
    multiply(3)
    multiply(4)
    gather(1)
    gather(2)

    forward(0, 2, 0)
    w_arrival(1, 2, 0).wait_recv()
    forward(1, 2, 1)
    w_arrival(0, 2, 1).wait_recv()
    multiply(5)
    multiply(6)

    own_n.wait()
    own_v.wait()
    remote(vst, vt.at[q_core], v_ssem.at[1], v_rsem.at[1], core_mate).wait_recv()
    remote(vst, vt.at[q_cross], v_ssem.at[2], v_rsem.at[2], core_mate).wait_recv()
    partial_sums(0)
    rs_step(0, 0)
    gather(3)
    gather(4)
    w_arrival(0, 3, 0).wait_recv()
    w_arrival(1, 3, 1).wait_recv()
    multiply(7)
    last_n = (n_copy(1, q_chip, chip_mate, 3), n_copy(2, q_cross, cross_mate, 3))
    for copy in last_n:
        copy.start()
    rs_step(0, 1)
    gather(5)
    gather(6)
    gather(7)

    mean = jnp.sum(s2[...], axis=1, keepdims=True) / WIDTH
    inv_one = invb[...]
    back_send[...] = inv_one * inv_one * inv_one * mean

    def back_copy():
        return to(back_send, back_recv, b_ssem.at[0], b_rsem.at[0], below_p, d)

    @pl.when(early_sender)
    def _():
        back_copy().start()

    def slots(i):
        return [(i * 4 + yy * 2 + cc, at(yy, zz(OFFSETS[i]), cc)) for yy in range(2) for cc in range(2)]

    def finish(slot, j):
        cols = chunk_cols(j)
        scaled = gf[:, cols].astype(F32) * nc[j].astype(F32)
        v = og[:, cols].astype(F32) + twice(invb) * scaled - xf[:, cols].astype(F32) * twice(back_send)
        fin[slot] = v.astype(BF16)

    def c_copy(slot, j, pipe, dev):
        return to(fin.at[slot], cot_out.at[:, chunk_cols(j)], c_ssem.at[slot], c_rsem.at[slot], pipe, dev)

    def rl_copy(slot):
        return to(fin.at[slot], relay.at[slot], rl_ssem.at[slot], rl_rsem.at[slot], 0, chip_mate)

    def on_copy(slot, j):
        return to(relay.at[slot], cot_out.at[:, chunk_cols(j)], c_ssem.at[slot], c_rsem.at[slot], mid - 1, chip_mate)

    @pl.when(p == mid)
    def _():
        for i in range(EARLY):
            for slot, j in slots(i):
                finish(slot, j)
                rl_copy(slot).start()
        for copy in last_n:
            copy.wait_send()

    for i in range(EARLY, RING):
        for slot, j in slots(i):
            finish(slot, j)

            @pl.when(p > 0)
            def _():
                c_copy(slot, j, below_p, d).start()

    rs_step(0, 2)
    partial_sums(1)
    rs_step(1, 0)
    rs_step(0, 3)
    for s in range(1, RING - 1):
        rs_step(1, s)
        if s + 3 < RING - 1:
            rs_step(0, s + 3)
        elif s + 3 == RING - 1:
            rs_end(0)
        if s <= EARLY:
            i = s - 1

            @pl.when(early_receiver)
            def _():
                if i == 0:
                    back_copy().wait_recv()
                for yy in range(2):
                    x_copy(i, yy).wait_recv()
                for slot, j in slots(i):
                    a_copy(slot).wait_recv()
                    half_cols = pl.ds((slot % 2) * CHUNK, CHUNK)
                    v = ar[slot].astype(F32) - xr[slot // 2, :, half_cols].astype(F32) * twice(back_recv)
                    cot_out[:, chunk_cols(j)] = v.astype(BF16)

            @pl.when(p == 0)
            def _():
                for slot, j in slots(i):
                    rl_copy(slot).wait_recv()
                    on_copy(slot, j).start()
    rs_end(1)

    @pl.when(p == sections - 1)
    def _():
        cot_out[...] = jnp.zeros_like(cot_out)

    @pl.when(p < sections - 1)
    def _():
        for i in range(EARLY, RING):
            for slot, j in slots(i):
                c_copy(slot, j, below_p, d).wait_recv()

    @pl.when(p == mid - 1)
    def _():
        for i in range(EARLY):
            for slot, j in slots(i):
                c_copy(slot, j, below_p, d).wait_recv()

    @pl.when(early_sender)
    def _():
        back_copy().wait_send()
        for i in range(EARLY):
            for yy in range(2):
                x_copy(i, yy).wait_send()
            for slot, j in slots(i):
                a_copy(slot).wait_send()

    @pl.when(p == mid)
    def _():
        for slot in range(4 * EARLY):
            rl_copy(slot).wait_send()

    @pl.when(p != mid)
    def _():
        for copy in last_n:
            copy.wait_send()

    @pl.when(p == 0)
    def _():
        for i in range(EARLY):
            for slot, j in slots(i):
                on_copy(slot, j).wait_send()

    @pl.when(p > 0)
    def _():
        for i in range(EARLY, RING):
            for slot, j in slots(i):
                c_copy(slot, j, below_p, d).wait_send()

    for copy in sent:
        copy.wait_send()


def shards(sections, *args):
    args = [a[0] if a.ndim == 3 else a for a in args]
    any_space = pl.BlockSpec(memory_space=pl.ANY)
    dma = pltpu.SemaphoreType.DMA
    cot, vg = pl.pallas_call(
        functools.partial(kernel, sections),
        out_shape=(
            jax.ShapeDtypeStruct((ROWS, WIDTH), BF16),
            jax.ShapeDtypeStruct((CHUNK, VW), F32),
        ),
        in_specs=[any_space] * 11,
        out_specs=(pl.BlockSpec(memory_space=pltpu.VMEM),) * 2,
        scratch_shapes=[
            pltpu.VMEM((ROWS, WIDTH), BF16),
            pltpu.VMEM((1, WIDTH), BF16),
            pltpu.VMEM((ROWS, 4096), BF16),
            pltpu.VMEM((ROWS, VW), BF16),
            pltpu.VMEM((ROWS, 4096), BF16),
            pltpu.VMEM((1, ROWS), jnp.int32),
            pltpu.VMEM((ROWS, WIDTH), BF16),
            pltpu.VMEM((1, WIDTH), BF16),
            pltpu.VMEM((ROWS, WIDTH), BF16),
            pltpu.VMEM((TEAM, ROWS, KW), BF16),
            pltpu.VMEM((RING, CHUNK, KW), BF16),
            pltpu.VMEM((RING, TEAM, ROWS, CHUNK), BF16),
            pltpu.VMEM((CHUNKS, ROWS, CHUNK), BF16),
            pltpu.VMEM((TEAM, ROWS, QUARTER), BF16),
            pltpu.VMEM((TEAM, ROWS, QUARTER), BF16),
            pltpu.VMEM((ROWS, VW), BF16),
            pltpu.VMEM((TEAM, ROWS, VW), BF16),
            pltpu.VMEM((2, RING, 128, VW), F32),
            pltpu.VMEM((2, RING - 1, SUBS, SUBROWS, VW), BF16),
            pltpu.VMEM((2, RING - 1, SUBS, SUBROWS, VW), BF16),
            pltpu.VMEM((CHUNKS, ROWS, CHUNK), BF16),
            pltpu.VMEM((4 * EARLY, ROWS, CHUNK), BF16),
            pltpu.VMEM((4 * EARLY, ROWS, CHUNK), BF16),
            pltpu.VMEM((2 * EARLY, ROWS, 2 * CHUNK), BF16),
            pltpu.VMEM((4 * EARLY, ROWS, CHUNK), BF16),
            pltpu.VMEM((ROWS, 128), F32),
            pltpu.VMEM((ROWS, 128), F32),
            pltpu.VMEM((ROWS, 128), F32),
            pltpu.VMEM((ROWS, 128), F32),
            pltpu.VMEM((ROWS, 128), F32),
            dma((11,)),
            dma((3,)), dma((3,)),
            dma((2, 7)), dma((2, 7)),
            dma((RING, 3)), dma((3, RING)),
            dma((3, PARTS)), dma((3, PARTS)),
            dma((3,)), dma((3,)),
            dma((2, RING - 1, SUBS)), dma((2, RING - 1, SUBS)),
            dma((CHUNKS,)), dma((CHUNKS,)),
            dma((2 * EARLY,)), dma((2 * EARLY,)),
            dma((4 * EARLY,)), dma((4 * EARLY,)),
            dma((1,)), dma((1,)),
            dma((4 * EARLY,)), dma((4 * EARLY,)),
            dma((2,)),
        ],
        compiler_params=pltpu.CompilerParams(
            collective_id=0, has_side_effects=True, vmem_limit_bytes=60 * 1024 * 1024),
        cost_estimate=pl.CostEstimate(flops=6_000_000_000, bytes_accessed=20_000_000, transcendentals=600_000),
    )(*args)
    return cot[None], vg[None]


def solution(mesh):
    placed = (
        P("pipe", "dp", None),
        P("pipe", None),
        P("pipe", "dp", None),
        P("pipe", "dp", None),
        P("pipe", "dp", None),
        P("pipe", "dp"),
        P("pipe", "dp", None),
        P("pipe", None),
        P("pipe", "dp", None),
        P("pipe", "dp", None),
        P("pipe", "dp", None),
    )
    return jax.shard_map(
        functools.partial(shards, mesh.shape["pipe"]),
        mesh=mesh,
        in_specs=placed,
        out_specs=(P("pipe", "dp", None), P("pipe", "dp", None)),
        check_vma=False,
    )
```

```python
import functools
import math

import jax
import jax.numpy as jnp
from jax import lax
from jax.experimental import pallas as pl
from jax.experimental.pallas import tpu as pltpu
from jax.sharding import PartitionSpec as P

HEAD = 128
NORM_EPS = 1e-05
MASKED = -1e30

MESH = pl.DeviceIdType.MESH
F32 = jnp.float32
BF16 = jnp.bfloat16

RING = 8
TEAM = 4
ROWS = 128
WIDTH = 8192
CHUNK = 256
CHUNKS = 32
QUARTER = 2048
VW = 512
KW = 1024
PARTS = 4
SUBS = 4
SUBROWS = 128 // SUBS
STEPS = RING // 2
OFFSETS = (0, -1, 1, -2, 2, -3, 3, 4)
EARLY = 4
DIRECT = 2


def kernel(
    sections,
    x_new, g_new, q_in, k_in, ctx_in, seg_in, x_frz, g_frz, og_in, kv_in, w_in,
    cot_out, vg_out,
    xn, gn, qv, kk, cx, sg, xf, gf, og, kvt, wbuf, rst, nc, nst, nt, vst, vt,
    pblk, rs_send, rs_recv, fin, ast, ar, xr, relay, back_send, back_recv, invb, s2, sq,
    load_sem, kv_ssem, kv_rsem, w_ssem, w_rsem, r_ssem, nc_rsem, n_ssem, n_rsem,
    v_ssem, v_rsem, rs_ssem, rs_rsem, c_ssem, c_rsem, x_ssem, x_rsem, a_ssem, a_rsem,
    b_ssem, b_rsem, rl_ssem, rl_rsem, on_ssem, own_sem,
):
    p = lax.axis_index("pipe")
    d = lax.axis_index("dp")
    y = d // 16
    z = (d // 2) % RING
    c = d % 2
    q = y * 2 + c

    def at(yy, zz, cc):
        return yy * 16 + zz * 2 + cc

    right = at(y, (z + 1) % RING, c)
    left = at(y, (z + RING - 1) % RING, c)
    core_mate = at(y, z, 1 - c)
    chip_mate = at(1 - y, z, c)
    cross_mate = at(1 - y, z, 1 - c)

    def remote(src, dst, ssem, rsem, dev):
        return pltpu.make_async_remote_copy(
            src_ref=src, dst_ref=dst, send_sem=ssem, recv_sem=rsem,
            device_id={"dp": dev}, device_id_type=MESH)

    mid = sections // 2
    below_p = lax.rem(p + sections - 1, sections)
    early_sender = (p > 0) & (p != mid)
    early_receiver = (p < sections - 1) & (p != mid - 1)

    def to(src, dst, ssem, rsem, pipe, dev):
        return pltpu.make_async_remote_copy(
            src_ref=src, dst_ref=dst, send_sem=ssem, recv_sem=rsem,
            device_id={"pipe": pipe, "dp": dev}, device_id_type=MESH)

    def signal(pipe, dev):
        pl.semaphore_signal(barrier, inc=1, device_id={"pipe": pipe, "dp": dev}, device_id_type=MESH)

    loads = [
        pltpu.make_async_copy(x_new, xn, load_sem.at[0]),
        pltpu.make_async_copy(g_new, gn, load_sem.at[1]),
        pltpu.make_async_copy(seg_in, sg, load_sem.at[2]),
        pltpu.make_async_copy(k_in, kk, load_sem.at[3]),
        pltpu.make_async_copy(q_in, qv, load_sem.at[4]),
        pltpu.make_async_copy(ctx_in, cx, load_sem.at[5]),
        pltpu.make_async_copy(kv_in, kvt.at[q], load_sem.at[6]),
        pltpu.make_async_copy(w_in, wbuf.at[z], load_sem.at[7]),
        pltpu.make_async_copy(x_frz, xf, load_sem.at[8]),
        pltpu.make_async_copy(g_frz, gf, load_sem.at[9]),
        pltpu.make_async_copy(og_in, og, load_sem.at[10]),
    ]
    for load in loads:
        load.start()

    barrier = pltpu.get_barrier_semaphore()
    for dev in (right, left, core_mate, chip_mate, cross_mate):
        pl.semaphore_signal(barrier, inc=1, device_id={"dp": dev}, device_id_type=MESH)

    @pl.when(p > 0)
    def _():
        signal(below_p, d)

    @pl.when(p < sections - 1)
    def _():
        signal(lax.rem(p + 1, sections), d)

    @pl.when(p == mid)
    def _():
        signal(0, chip_mate)
        signal(mid - 1, chip_mate)

    @pl.when(p == 0)
    def _():
        signal(mid, chip_mate)
        signal(mid - 1, chip_mate)

    @pl.when(p == mid - 1)
    def _():
        signal(0, chip_mate)
        signal(mid, chip_mate)

    pl.semaphore_wait(
        barrier,
        5 + jnp.where(p > 0, 1, 2) + jnp.where(p < sections - 1, 1, 0)
        + jnp.where((p == mid) | (p == mid - 1), 2, 0))

    def half(slot, h):
        return wbuf.at[slot, pl.ds(h * 128, 128)]

    def zz(k):
        return (z + RING + k) % RING

    def w_copy(way, k, h, own=False):
        slot = zz(-k) if way == 0 else zz(k)
        n = 2 * k + (h if k < 3 else 0)
        src = w_in.at[pl.ds(h * 128, 128)] if own else half(slot, h)
        return remote(src, half(slot, h), w_ssem.at[way, n], w_rsem.at[way, n], right if way == 0 else left)

    def w_arrival(way, k, h):
        slot = zz(-(k + 1)) if way == 0 else zz(k + 1)
        n = 2 * k + (h if k < 3 else 0)
        return remote(half(slot, h), half(slot, h), w_ssem.at[way, n], w_rsem.at[way, n], right if way == 0 else left)

    sent = []

    def start(copy):
        copy.start()
        sent.append(copy)

    for h in range(2):
        start(w_copy(0, 0, h, own=True))
        start(w_copy(1, 0, h, own=True))

    start(remote(kv_in, kvt.at[q], kv_ssem.at[0], kv_rsem.at[0], chip_mate))
    start(remote(kv_in, kvt.at[q], kv_ssem.at[1], kv_rsem.at[1], core_mate))

    def chunk_cols(j):
        return pl.ds(pl.multiple_of(j * CHUNK, CHUNK), CHUNK)

    def x_copy(i, yy):
        cols = pl.ds(pl.multiple_of(at(yy, zz(OFFSETS[i]), 0) * CHUNK, 2 * CHUNK), 2 * CHUNK)
        return to(x_frz.at[:, cols], xr.at[i * 2 + yy], x_ssem.at[i * 2 + yy], x_rsem.at[i * 2 + yy], below_p, d)

    @pl.when(early_sender)
    def _():
        for i in range(EARLY):
            for yy in range(2):
                x_copy(i, yy).start()

    q_core = y * 2 + (1 - c)
    q_chip = (1 - y) * 2 + c
    q_cross = (1 - y) * 2 + (1 - c)

    loads[0].wait()
    loads[1].wait()
    sq[...] = jnp.zeros_like(sq)

    @pl.loop(0, CHUNKS)
    def _(j):
        v = xn[:, pl.ds(pl.multiple_of(j * CHUNK, CHUNK), CHUNK)].astype(F32)
        v = v * v
        sq[...] += v[:, :128] + v[:, 128:]

    inv_new = lax.rsqrt(jnp.sum(sq[...], axis=1, keepdims=True) / WIDTH + NORM_EPS)

    @pl.loop(0, CHUNKS)
    def _(j):
        cols = pl.ds(pl.multiple_of(j * CHUNK, CHUNK), CHUNK)
        v = xn[:, cols].astype(F32) * inv_new * gn[:, cols].astype(F32)
        role = (j // 16) * 2 + j % 2
        block = ((j // 2) % RING) * 128
        v = v.astype(BF16)
        nst[role, :, pl.ds(pl.multiple_of(block, 128), 128)] = v[:, :128]
        nst[role, :, pl.ds(pl.multiple_of(block + RING * 128, 128), 128)] = v[:, 128:]

    def n_copy(index, role, dev, part):
        cols = pl.ds(part * (QUARTER // PARTS), QUARTER // PARTS)
        return remote(nst.at[role, :, cols], nt.at[q, :, cols], n_ssem.at[index, part], n_rsem.at[index, part], dev)

    def n_part(part):
        start(n_copy(1, q_chip, chip_mate, part))
        start(n_copy(2, q_cross, cross_mate, part))

    own_n = pltpu.make_async_copy(nst.at[q], nt.at[q], own_sem.at[0])
    own_n.start()
    n_part(0)
    for part in range(PARTS):
        start(n_copy(0, q_core, core_mate, part))

    def forward(way, k, h):
        w_arrival(way, k, h).wait_recv()
        start(w_copy(way, k + 1, h))

    n_part(1)

    forward(0, 0, 0)
    forward(1, 0, 0)

    remote(kv_in, kvt.at[q_chip], kv_ssem.at[0], kv_rsem.at[0], chip_mate).wait_recv()
    start(remote(kvt.at[q_chip], kvt.at[q_chip], kv_ssem.at[2], kv_rsem.at[2], core_mate))

    for load in loads[2:6]:
        load.wait()
    seg_i = jnp.broadcast_to(sg[...].astype(F32), (ROWS, ROWS))
    seg_j = seg_i.T
    pos_j = lax.broadcasted_iota(jnp.int32, (ROWS, ROWS), 0)
    pos_i = lax.broadcasted_iota(jnp.int32, (ROWS, ROWS), 1)
    visible_one = jnp.where((seg_i == seg_j) & (pos_j <= pos_i), 1.0, 0.0)
    scale = 1.0 / math.sqrt(HEAD)

    @pl.loop(0, 4)
    def _(g):
        keys = kk[:, pl.ds(pl.multiple_of(g * HEAD, HEAD), HEAD)]
        total = jnp.zeros((ROWS, HEAD), F32)
        for h in range(8):
            cols = pl.ds(pl.multiple_of(g * 8 * HEAD + h * HEAD, HEAD), HEAD)
            s = lax.dot_general(keys, qv[:, cols], (((1,), (1,)), ((), ())), preferred_element_type=F32) * scale
            seen = visible_one > 0.5
            s = jnp.where(seen, s, MASKED)
            top = jnp.max(s, axis=0, keepdims=True)
            e = jnp.where(seen, jnp.exp(s - top), 0.0)
            a = (e / jnp.sum(e, axis=0, keepdims=True)).astype(BF16)
            total += jnp.dot(a, cx[:, cols], preferred_element_type=F32)
        vst[:, pl.ds(pl.multiple_of(g * HEAD, HEAD), HEAD)] = total.astype(BF16)

    start(remote(vst, vt.at[q], v_ssem.at[0], v_rsem.at[0], chip_mate))
    start(remote(vst, vt.at[q], v_ssem.at[1], v_rsem.at[1], core_mate))
    own_v = pltpu.make_async_copy(vst, vt.at[q], own_sem.at[1])
    own_v.start()

    forward(0, 0, 1)
    forward(1, 0, 1)

    for load in loads[6:11]:
        load.wait()
    remote(kv_in, kvt.at[q_core], kv_ssem.at[1], kv_rsem.at[1], core_mate).wait_recv()
    remote(kv_in, kvt.at[q_cross], kv_ssem.at[2], kv_rsem.at[2], core_mate).wait_recv()

    s2[...] = jnp.zeros_like(s2)
    sq[...] = jnp.zeros_like(sq)

    @pl.loop(0, CHUNKS)
    def _(j):
        v = xf[:, chunk_cols(j)].astype(F32)
        v = v * v
        sq[...] += v[:, :128] + v[:, 128:]

    inv_frz = lax.rsqrt(jnp.sum(sq[...], axis=1, keepdims=True) / WIDTH + NORM_EPS)
    invb[...] = jnp.broadcast_to(inv_frz, (ROWS, 128))

    def twice(ref):
        v = ref[...]
        return jnp.concatenate([v, v], axis=1)

    def a_copy(slot):
        return to(ast.at[slot], ar.at[slot], a_ssem.at[slot], a_rsem.at[slot], below_p, d)

    def accumulate(i, yy, cc):
        j = at(yy, zz(OFFSETS[i]), cc)
        cols = chunk_cols(j)
        scaled = gf[:, cols].astype(F32) * nc[j].astype(F32)
        v = xf[:, cols].astype(F32) * scaled
        s2[...] += v[:, :128] + v[:, 128:]
        if i < EARLY:
            slot = i * 4 + yy * 2 + cc
            ast[slot] = (og[:, cols].astype(F32) + twice(invb) * scaled).astype(BF16)

            @pl.when(early_sender)
            def _():
                a_copy(slot).start()

    def result_copy(slot, index, role, dev):
        j = at(y, slot, c)
        return remote(rst.at[slot, role], nc.at[j], r_ssem.at[slot, index], nc_rsem.at[index, slot], dev)

    def multiply(i):
        slot = zz(OFFSETS[i])
        w = wbuf[slot]
        for m in range(2):
            kv = kvt[pl.ds(2 * m, 2)].reshape(2 * ROWS, KW)
            r = lax.dot_general(kv, w, (((1,), (1,)), ((), ())), preferred_element_type=F32)
            rst[slot, pl.ds(2 * m, 2)] = r.astype(BF16).reshape(2, ROWS, CHUNK)
        start(result_copy(slot, 1, q_chip, chip_mate))
        start(result_copy(slot, 2, q_cross, cross_mate))
        start(result_copy(slot, 0, q_core, core_mate))
        nc[at(y, slot, c)] = rst[slot, q]
        accumulate(i, y, c)

    def gather(i):
        slot = zz(OFFSETS[i])
        for index, (yy, cc) in ((0, (y, 1 - c)), (1, (1 - y, c)), (2, (1 - y, 1 - c))):
            j = at(yy, slot, cc)
            remote(rst.at[slot, 0], nc.at[j], r_ssem.at[slot, index], nc_rsem.at[index, slot], chip_mate).wait_recv()
            accumulate(i, yy, cc)

    def partial_sums(way):
        for index, role in ((0, q_core), (1, q_chip), (2, q_cross)):
            for part in (2 * way, 2 * way + 1):
                cols = pl.ds(part * (QUARTER // PARTS), QUARTER // PARTS)
                remote(nst.at[0, :, cols], nt.at[role, :, cols], n_ssem.at[index, part], n_rsem.at[index, part], core_mate).wait_recv()

        @pl.loop(0, RING // 2)
        def _(i):
            cols = pl.ds(pl.multiple_of(way * RING * 128 + i * 256, 256), 256)
            rows = nt[:, :, cols].reshape(TEAM * ROWS, 256)
            r = lax.dot_general(rows, vt[...].reshape(TEAM * ROWS, VW), (((0,), (0,)), ((), ())), preferred_element_type=F32)
            pblk[way, pl.ds(2 * i, 2)] = r.reshape(2, 128, VW)

    def rs_copy(way, side, sub, s):
        return remote(
            rs_send.at[way, side, s, sub], rs_recv.at[way, side, s, sub], rs_ssem.at[way, side, s, sub],
            rs_rsem.at[way, side, s, sub], right if side == 0 else left)

    def first_step(side, sub):
        return 0 if (sub < SUBS // 2) == (side == 0) else 1

    def rs_step(way, s):
        for fresh in (True, False):
            for sub in range(SUBS):
                for side in range(2):
                    start_at = first_step(side, sub)
                    if s < start_at or (s == start_at) != fresh:
                        continue
                    b = zz(4 - s) if side == 0 else zz(s - 4)
                    v = pblk[way, b, pl.ds(sub * SUBROWS, SUBROWS)]
                    if s > start_at:
                        rs_copy(way, side, sub, s - 1).wait_recv()
                        v += rs_recv[way, side, s - 1, sub].astype(F32)
                    rs_send[way, side, s, sub] = v.astype(BF16)
                    start(rs_copy(way, side, sub, s))

    def rs_end(way):
        for sub in range(SUBS):
            v = pblk[way, z, pl.ds(sub * SUBROWS, SUBROWS)]
            for side in range(2):
                rs_copy(way, side, sub, STEPS - 1).wait_recv()
                v += rs_recv[way, side, STEPS - 1, sub].astype(F32)
            vg_out[pl.ds(way * 128 + sub * SUBROWS, SUBROWS)] = v

    multiply(0)
    multiply(1)
    multiply(2)
    n_part(2)

    remote(vst, vt.at[q_chip], v_ssem.at[0], v_rsem.at[0], chip_mate).wait_recv()
    start(remote(vt.at[q_chip], vt.at[q_chip], v_ssem.at[2], v_rsem.at[2], core_mate))

    forward(0, 1, 0)
    forward(1, 1, 0)
    gather(0)
    forward(0, 1, 1)
    forward(1, 1, 1)
    multiply(3)
    multiply(4)
    gather(1)
    gather(2)

    forward(0, 2, 0)
    w_arrival(1, 2, 0).wait_recv()
    forward(1, 2, 1)
    w_arrival(0, 2, 1).wait_recv()
    multiply(5)
    multiply(6)

    own_n.wait()
    own_v.wait()
    remote(vst, vt.at[q_core], v_ssem.at[1], v_rsem.at[1], core_mate).wait_recv()
    remote(vst, vt.at[q_cross], v_ssem.at[2], v_rsem.at[2], core_mate).wait_recv()
    partial_sums(0)
    rs_step(0, 0)
    gather(3)
    gather(4)
    w_arrival(0, 3, 0).wait_recv()
    w_arrival(1, 3, 1).wait_recv()
    multiply(7)
    n_part(3)
    rs_step(0, 1)
    gather(5)
    gather(6)
    gather(7)

    mean = jnp.sum(s2[...], axis=1, keepdims=True) / WIDTH
    inv_one = invb[...]
    back_send[...] = inv_one * inv_one * inv_one * mean

    def back_copy():
        return to(back_send, back_recv, b_ssem.at[0], b_rsem.at[0], below_p, d)

    @pl.when(early_sender)
    def _():
        back_copy().start()

    def slots(i):
        return [(i * 4 + yy * 2 + cc, at(yy, zz(OFFSETS[i]), cc)) for yy in range(2) for cc in range(2)]

    def finish(slot, j):
        cols = chunk_cols(j)
        scaled = gf[:, cols].astype(F32) * nc[j].astype(F32)
        v = og[:, cols].astype(F32) + twice(invb) * scaled - xf[:, cols].astype(F32) * twice(back_send)
        fin[slot] = v.astype(BF16)

    def c_copy(slot, j, pipe, dev):
        return to(fin.at[slot], cot_out.at[:, chunk_cols(j)], c_ssem.at[slot], c_rsem.at[slot], pipe, dev)

    def rl_copy(slot):
        n = slot % (4 * EARLY)
        return to(fin.at[slot], relay.at[n], rl_ssem.at[slot], rl_rsem.at[n], 0 if slot < 4 * EARLY else mid, chip_mate)

    def on_copy(slot, j):
        return to(relay.at[slot % (4 * EARLY)], cot_out.at[:, chunk_cols(j)], on_ssem.at[slot % (4 * EARLY)], c_rsem.at[slot], mid - 1, chip_mate)

    @pl.when(p == mid)
    def _():
        for i in range(EARLY):
            for late in range(0, RING - DIRECT, EARLY):
                if i + late < RING - DIRECT:
                    for slot, j in slots(i + late):
                        finish(slot, j)
                        rl_copy(slot).start()
        for i in range(RING - DIRECT, RING):
            for slot, j in slots(i):
                finish(slot, j)

    @pl.when(p != mid)
    def _():
        for i in range(EARLY, RING):
            for slot, j in slots(i):
                finish(slot, j)

                @pl.when(p > 0)
                def _():
                    c_copy(slot, j, below_p, d).start()

    rs_step(0, 2)

    def correct(i):
        @pl.when(early_receiver)
        def _():
            if i == 0:
                back_copy().wait_recv()
            for yy in range(2):
                x_copy(i, yy).wait_recv()
            for slot, j in slots(i):
                a_copy(slot).wait_recv()
                half_cols = pl.ds((slot % 2) * CHUNK, CHUNK)
                v = ar[slot].astype(F32) - xr[slot // 2, :, half_cols].astype(F32) * twice(back_recv)
                cot_out[:, chunk_cols(j)] = v.astype(BF16)

    def pass_on(i):
        @pl.when(p == 0)
        def _():
            for slot, j in slots(i):
                rl_copy(slot).wait_recv()
                on_copy(slot, j).start()

        if i + EARLY < RING - DIRECT:
            @pl.when(p == mid)
            def _():
                for slot, j in slots(i + EARLY):
                    rl_copy(slot).wait_recv()
                    on_copy(slot, j).start()

    rs_step(0, 3)
    partial_sums(1)
    rs_step(1, 0)

    @pl.when(p == mid)
    def _():
        for i in range(RING - DIRECT, RING):
            for slot, j in slots(i):
                c_copy(slot, j, below_p, d).start()

    rs_end(0)
    pass_on(0)
    rs_step(1, 1)
    correct(0)
    pass_on(1)
    rs_step(1, 2)
    correct(1)
    pass_on(2)
    rs_step(1, 3)
    correct(2)
    correct(3)
    pass_on(3)
    rs_end(1)

    @pl.when(p == sections - 1)
    def _():
        cot_out[...] = jnp.zeros_like(cot_out)

    @pl.when(p < sections - 1)
    def _():
        for i in range(EARLY, RING):
            for slot, j in slots(i):
                c_copy(slot, j, below_p, d).wait_recv()

    @pl.when(p == mid - 1)
    def _():
        for i in range(EARLY):
            for slot, j in slots(i):
                c_copy(slot, j, below_p, d).wait_recv()

    @pl.when(early_sender)
    def _():
        back_copy().wait_send()
        for i in range(EARLY):
            for yy in range(2):
                x_copy(i, yy).wait_send()
            for slot, j in slots(i):
                a_copy(slot).wait_send()

    @pl.when(p == mid)
    def _():
        for i in range(RING - DIRECT):
            for slot, j in slots(i):
                rl_copy(slot).wait_send()
        for i in range(EARLY, RING):
            for slot, j in slots(i):
                if i < RING - DIRECT:
                    on_copy(slot, j).wait_send()
                else:
                    c_copy(slot, j, below_p, d).wait_send()

    @pl.when(p == 0)
    def _():
        for i in range(EARLY):
            for slot, j in slots(i):
                on_copy(slot, j).wait_send()

    @pl.when(early_sender)
    def _():
        for i in range(EARLY, RING):
            for slot, j in slots(i):
                c_copy(slot, j, below_p, d).wait_send()

    for copy in sent:
        copy.wait_send()


def shards(sections, *args):
    args = [a[0] if a.ndim == 3 else a for a in args]
    any_space = pl.BlockSpec(memory_space=pl.ANY)
    dma = pltpu.SemaphoreType.DMA
    cot, vg = pl.pallas_call(
        functools.partial(kernel, sections),
        out_shape=(
            jax.ShapeDtypeStruct((ROWS, WIDTH), BF16),
            jax.ShapeDtypeStruct((CHUNK, VW), F32),
        ),
        in_specs=[any_space] * 11,
        out_specs=(pl.BlockSpec(memory_space=pltpu.VMEM),) * 2,
        scratch_shapes=[
            pltpu.VMEM((ROWS, WIDTH), BF16),
            pltpu.VMEM((1, WIDTH), BF16),
            pltpu.VMEM((ROWS, 4096), BF16),
            pltpu.VMEM((ROWS, VW), BF16),
            pltpu.VMEM((ROWS, 4096), BF16),
            pltpu.VMEM((1, ROWS), jnp.int32),
            pltpu.VMEM((ROWS, WIDTH), BF16),
            pltpu.VMEM((1, WIDTH), BF16),
            pltpu.VMEM((ROWS, WIDTH), BF16),
            pltpu.VMEM((TEAM, ROWS, KW), BF16),
            pltpu.VMEM((RING, CHUNK, KW), BF16),
            pltpu.VMEM((RING, TEAM, ROWS, CHUNK), BF16),
            pltpu.VMEM((CHUNKS, ROWS, CHUNK), BF16),
            pltpu.VMEM((TEAM, ROWS, QUARTER), BF16),
            pltpu.VMEM((TEAM, ROWS, QUARTER), BF16),
            pltpu.VMEM((ROWS, VW), BF16),
            pltpu.VMEM((TEAM, ROWS, VW), BF16),
            pltpu.VMEM((2, RING, 128, VW), F32),
            pltpu.VMEM((2, 2, STEPS, SUBS, SUBROWS, VW), BF16),
            pltpu.VMEM((2, 2, STEPS, SUBS, SUBROWS, VW), BF16),
            pltpu.VMEM((CHUNKS, ROWS, CHUNK), BF16),
            pltpu.VMEM((4 * EARLY, ROWS, CHUNK), BF16),
            pltpu.VMEM((4 * EARLY, ROWS, CHUNK), BF16),
            pltpu.VMEM((2 * EARLY, ROWS, 2 * CHUNK), BF16),
            pltpu.VMEM((4 * EARLY, ROWS, CHUNK), BF16),
            pltpu.VMEM((ROWS, 128), F32),
            pltpu.VMEM((ROWS, 128), F32),
            pltpu.VMEM((ROWS, 128), F32),
            pltpu.VMEM((ROWS, 128), F32),
            pltpu.VMEM((ROWS, 128), F32),
            dma((11,)),
            dma((3,)), dma((3,)),
            dma((2, 7)), dma((2, 7)),
            dma((RING, 3)), dma((3, RING)),
            dma((3, PARTS)), dma((3, PARTS)),
            dma((3,)), dma((3,)),
            dma((2, 2, STEPS, SUBS)), dma((2, 2, STEPS, SUBS)),
            dma((CHUNKS,)), dma((CHUNKS,)),
            dma((2 * EARLY,)), dma((2 * EARLY,)),
            dma((4 * EARLY,)), dma((4 * EARLY,)),
            dma((1,)), dma((1,)),
            dma((CHUNKS,)), dma((4 * EARLY,)), dma((4 * EARLY,)),
            dma((2,)),
        ],
        compiler_params=pltpu.CompilerParams(
            collective_id=0, has_side_effects=True, vmem_limit_bytes=60 * 1024 * 1024),
        cost_estimate=pl.CostEstimate(flops=6_000_000_000, bytes_accessed=20_000_000, transcendentals=600_000),
    )(*args)
    return cot[None], vg[None]


def solution(mesh):
    placed = (
        P("pipe", "dp", None),
        P("pipe", None),
        P("pipe", "dp", None),
        P("pipe", "dp", None),
        P("pipe", "dp", None),
        P("pipe", "dp"),
        P("pipe", "dp", None),
        P("pipe", None),
        P("pipe", "dp", None),
        P("pipe", "dp", None),
        P("pipe", "dp", None),
    )
    return jax.shard_map(
        functools.partial(shards, mesh.shape["pipe"]),
        mesh=mesh,
        in_specs=placed,
        out_specs=(P("pipe", "dp", None), P("pipe", "dp", None)),
        check_vma=False,
    )
```

```python
import functools
import math

import jax
import jax.numpy as jnp
from jax import lax
from jax.experimental import pallas as pl
from jax.experimental.pallas import tpu as pltpu
from jax.sharding import PartitionSpec as P

HEAD = 128
NORM_EPS = 1e-05
MASKED = -1e30

MESH = pl.DeviceIdType.MESH
F32 = jnp.float32
BF16 = jnp.bfloat16

RING = 8
TEAM = 4
ROWS = 128
WIDTH = 8192
CHUNK = 256
CHUNKS = 32
QUARTER = 2048
VW = 512
KW = 1024
PARTS = 4
SUBS = 4
SUBROWS = 128 // SUBS
STEPS = RING // 2
OFFSETS = (0, -1, 1, -2, 2, -3, 3, 4)
EARLY = 4
EARLY_MID = 3
VIA_ZERO = (3, 6)
VIA_MATE = (4, 5)
DIRECT = (7,)
PLACES = 8


def kernel(
    sections,
    x_new, g_new, q_in, k_in, ctx_in, seg_in, x_frz, g_frz, og_in, kv_in, w_in,
    cot_out, vg_out,
    xn, gn, qv, kk, cx, sg, xf, gf, og, kvt, wbuf, rst, nc, nst, nt, vst, vt,
    pblk, rs_send, rs_recv, fin, ast, ar, xr, relay, back_send, back_recv, invb, s2, sq, vgb,
    load_sem, kv_ssem, kv_rsem, w_ssem, w_rsem, r_ssem, nc_rsem, n_ssem, n_rsem,
    v_ssem, v_rsem, rs_ssem, rs_rsem, c_ssem, c_rsem, x_ssem, x_rsem, a_ssem, a_rsem,
    b_ssem, b_rsem, rl_ssem, rl_rsem, on_ssem, own_sem, o_sem, zero_sem, vg_sem,
):
    p = lax.axis_index("pipe")
    d = lax.axis_index("dp")
    y = d // 16
    z = (d // 2) % RING
    c = d % 2
    q = y * 2 + c

    def at(yy, zz, cc):
        return yy * 16 + zz * 2 + cc

    right = at(y, (z + 1) % RING, c)
    left = at(y, (z + RING - 1) % RING, c)
    core_mate = at(y, z, 1 - c)
    chip_mate = at(1 - y, z, c)
    cross_mate = at(1 - y, z, 1 - c)
    early_dev = jnp.where(p == sections // 2, chip_mate, d)

    def remote(src, dst, ssem, rsem, dev):
        return pltpu.make_async_remote_copy(
            src_ref=src, dst_ref=dst, send_sem=ssem, recv_sem=rsem,
            device_id={"dp": dev}, device_id_type=MESH)

    mid = sections // 2
    below_p = lax.rem(p + sections - 1, sections)

    def sends_early(i):
        return (p > 0) & ((p != mid) | (i < EARLY_MID))

    def to(src, dst, ssem, rsem, pipe, dev):
        return pltpu.make_async_remote_copy(
            src_ref=src, dst_ref=dst, send_sem=ssem, recv_sem=rsem,
            device_id={"pipe": pipe, "dp": dev}, device_id_type=MESH)

    def signal(pipe, dev):
        pl.semaphore_signal(barrier, inc=1, device_id={"pipe": pipe, "dp": dev}, device_id_type=MESH)

    loads = [
        pltpu.make_async_copy(x_new, xn, load_sem.at[0]),
        pltpu.make_async_copy(g_new, gn, load_sem.at[1]),
        pltpu.make_async_copy(seg_in, sg, load_sem.at[2]),
        pltpu.make_async_copy(k_in, kk, load_sem.at[3]),
        pltpu.make_async_copy(q_in, qv, load_sem.at[4]),
        pltpu.make_async_copy(ctx_in, cx, load_sem.at[5]),
        pltpu.make_async_copy(kv_in, kvt.at[q], load_sem.at[6]),
        pltpu.make_async_copy(w_in, wbuf.at[z], load_sem.at[7]),
        pltpu.make_async_copy(x_frz, xf, load_sem.at[8]),
        pltpu.make_async_copy(g_frz, gf, load_sem.at[9]),
        pltpu.make_async_copy(og_in, og, load_sem.at[10]),
    ]
    for load in loads:
        load.start()

    barrier = pltpu.get_barrier_semaphore()
    for dev in (right, left, core_mate, chip_mate, cross_mate):
        pl.semaphore_signal(barrier, inc=1, device_id={"dp": dev}, device_id_type=MESH)

    @pl.when(p > 0)
    def _():
        signal(below_p, d)

    @pl.when(p < sections - 1)
    def _():
        signal(lax.rem(p + 1, sections), d)

    @pl.when(p == mid)
    def _():
        signal(0, chip_mate)
        signal(mid - 1, chip_mate)

    @pl.when(p == 0)
    def _():
        signal(mid, chip_mate)
        signal(mid - 1, d)

    @pl.when(p == mid - 1)
    def _():
        signal(0, d)
        signal(mid, chip_mate)

    pl.semaphore_wait(
        barrier,
        5 + jnp.where(p > 0, 1, 2) + jnp.where(p < sections - 1, 1, 0)
        + jnp.where((p == mid) | (p == mid - 1), 2, 0))

    def half(slot, h):
        return wbuf.at[slot, pl.ds(h * 128, 128)]

    def zz(k):
        return (z + RING + k) % RING

    def w_copy(way, k, h, own=False):
        slot = zz(-k) if way == 0 else zz(k)
        n = 2 * k + (h if k < 3 else 0)
        src = w_in.at[pl.ds(h * 128, 128)] if own else half(slot, h)
        return remote(src, half(slot, h), w_ssem.at[way, n], w_rsem.at[way, n], right if way == 0 else left)

    def w_arrival(way, k, h):
        slot = zz(-(k + 1)) if way == 0 else zz(k + 1)
        n = 2 * k + (h if k < 3 else 0)
        return remote(half(slot, h), half(slot, h), w_ssem.at[way, n], w_rsem.at[way, n], right if way == 0 else left)

    sent = []

    def start(copy):
        copy.start()
        sent.append(copy)

    for h in range(2):
        start(w_copy(0, 0, h, own=True))
        start(w_copy(1, 0, h, own=True))

    start(remote(kv_in, kvt.at[q], kv_ssem.at[0], kv_rsem.at[0], chip_mate))
    start(remote(kv_in, kvt.at[q], kv_ssem.at[1], kv_rsem.at[1], core_mate))

    def chunk_cols(j):
        return pl.ds(pl.multiple_of(j * CHUNK, CHUNK), CHUNK)

    def x_copy(i, yy):
        cols = pl.ds(pl.multiple_of(at(yy, zz(OFFSETS[i]), 0) * CHUNK, 2 * CHUNK), 2 * CHUNK)
        return to(x_frz.at[:, cols], xr.at[i * 2 + yy], x_ssem.at[i * 2 + yy], x_rsem.at[i * 2 + yy], below_p, early_dev)

    for i in range(EARLY):
        @pl.when(sends_early(i))
        def _():
            for yy in range(2):
                x_copy(i, yy).start()

    q_core = y * 2 + (1 - c)
    q_chip = (1 - y) * 2 + c
    q_cross = (1 - y) * 2 + (1 - c)

    loads[0].wait()
    loads[1].wait()
    sq[...] = jnp.zeros_like(sq)

    @pl.loop(0, CHUNKS)
    def _(j):
        v = xn[:, pl.ds(pl.multiple_of(j * CHUNK, CHUNK), CHUNK)].astype(F32)
        v = v * v
        sq[...] += v[:, :128] + v[:, 128:]

    inv_new = lax.rsqrt(jnp.sum(sq[...], axis=1, keepdims=True) / WIDTH + NORM_EPS)

    @pl.loop(0, CHUNKS)
    def _(j):
        cols = pl.ds(pl.multiple_of(j * CHUNK, CHUNK), CHUNK)
        v = xn[:, cols].astype(F32) * inv_new * gn[:, cols].astype(F32)
        role = (j // 16) * 2 + j % 2
        block = ((j // 2) % RING) * 128
        v = v.astype(BF16)
        nst[role, :, pl.ds(pl.multiple_of(block, 128), 128)] = v[:, :128]
        nst[role, :, pl.ds(pl.multiple_of(block + RING * 128, 128), 128)] = v[:, 128:]

    def n_copy(index, role, dev, part):
        cols = pl.ds(part * (QUARTER // PARTS), QUARTER // PARTS)
        return remote(nst.at[role, :, cols], nt.at[q, :, cols], n_ssem.at[index, part], n_rsem.at[index, part], dev)

    def n_part(part):
        start(n_copy(1, q_chip, chip_mate, part))
        start(n_copy(2, q_cross, cross_mate, part))

    own_n = pltpu.make_async_copy(nst.at[q], nt.at[q], own_sem.at[0])
    own_n.start()
    n_part(0)
    for part in range(PARTS):
        start(n_copy(0, q_core, core_mate, part))

    def forward(way, k, h):
        w_arrival(way, k, h).wait_recv()
        start(w_copy(way, k + 1, h))

    n_part(1)

    forward(0, 0, 0)
    forward(1, 0, 0)

    remote(kv_in, kvt.at[q_chip], kv_ssem.at[0], kv_rsem.at[0], chip_mate).wait_recv()
    start(remote(kvt.at[q_chip], kvt.at[q_chip], kv_ssem.at[2], kv_rsem.at[2], core_mate))

    for load in loads[2:6]:
        load.wait()
    seg_i = jnp.broadcast_to(sg[...].astype(F32), (ROWS, ROWS))
    seg_j = seg_i.T
    pos_j = lax.broadcasted_iota(jnp.int32, (ROWS, ROWS), 0)
    pos_i = lax.broadcasted_iota(jnp.int32, (ROWS, ROWS), 1)
    visible_one = jnp.where((seg_i == seg_j) & (pos_j <= pos_i), 1.0, 0.0)
    scale = 1.0 / math.sqrt(HEAD)

    @pl.loop(0, 4)
    def _(g):
        keys = kk[:, pl.ds(pl.multiple_of(g * HEAD, HEAD), HEAD)]
        total = jnp.zeros((ROWS, HEAD), F32)
        for h in range(8):
            cols = pl.ds(pl.multiple_of(g * 8 * HEAD + h * HEAD, HEAD), HEAD)
            s = lax.dot_general(keys, qv[:, cols], (((1,), (1,)), ((), ())), preferred_element_type=F32) * scale
            seen = visible_one > 0.5
            s = jnp.where(seen, s, MASKED)
            top = jnp.max(s, axis=0, keepdims=True)
            e = jnp.where(seen, jnp.exp(s - top), 0.0)
            a = (e / jnp.sum(e, axis=0, keepdims=True)).astype(BF16)
            total += jnp.dot(a, cx[:, cols], preferred_element_type=F32)
        vst[:, pl.ds(pl.multiple_of(g * HEAD, HEAD), HEAD)] = total.astype(BF16)

    start(remote(vst, vt.at[q], v_ssem.at[0], v_rsem.at[0], chip_mate))
    start(remote(vst, vt.at[q], v_ssem.at[1], v_rsem.at[1], core_mate))
    own_v = pltpu.make_async_copy(vst, vt.at[q], own_sem.at[1])
    own_v.start()

    forward(0, 0, 1)
    forward(1, 0, 1)

    for load in loads[6:11]:
        load.wait()
    remote(kv_in, kvt.at[q_core], kv_ssem.at[1], kv_rsem.at[1], core_mate).wait_recv()
    remote(kv_in, kvt.at[q_cross], kv_ssem.at[2], kv_rsem.at[2], core_mate).wait_recv()

    s2[...] = jnp.zeros_like(s2)
    sq[...] = jnp.zeros_like(sq)

    @pl.loop(0, CHUNKS)
    def _(j):
        v = xf[:, chunk_cols(j)].astype(F32)
        v = v * v
        sq[...] += v[:, :128] + v[:, 128:]

    inv_frz = lax.rsqrt(jnp.sum(sq[...], axis=1, keepdims=True) / WIDTH + NORM_EPS)
    invb[...] = jnp.broadcast_to(inv_frz, (ROWS, 128))

    def twice(ref):
        v = ref[...]
        return jnp.concatenate([v, v], axis=1)

    def a_copy(slot):
        return to(ast.at[slot], ar.at[slot], a_ssem.at[slot], a_rsem.at[slot], below_p, early_dev)

    def accumulate(i, yy, cc):
        j = at(yy, zz(OFFSETS[i]), cc)
        cols = chunk_cols(j)
        scaled = gf[:, cols].astype(F32) * nc[j].astype(F32)
        v = xf[:, cols].astype(F32) * scaled
        s2[...] += v[:, :128] + v[:, 128:]
        if i < EARLY:
            slot = i * 4 + yy * 2 + cc
            ast[slot] = (og[:, cols].astype(F32) + twice(invb) * scaled).astype(BF16)

            @pl.when(sends_early(i))
            def _():
                a_copy(slot).start()

    def result_copy(slot, index, role, dev):
        j = at(y, slot, c)
        return remote(rst.at[slot, role], nc.at[j], r_ssem.at[slot, index], nc_rsem.at[index, slot], dev)

    def multiply(i):
        slot = zz(OFFSETS[i])
        w = wbuf[slot]
        for m in range(2):
            kv = kvt[pl.ds(2 * m, 2)].reshape(2 * ROWS, KW)
            r = lax.dot_general(kv, w, (((1,), (1,)), ((), ())), preferred_element_type=F32)
            rst[slot, pl.ds(2 * m, 2)] = r.astype(BF16).reshape(2, ROWS, CHUNK)
        start(result_copy(slot, 1, q_chip, chip_mate))
        start(result_copy(slot, 2, q_cross, cross_mate))
        start(result_copy(slot, 0, q_core, core_mate))
        nc[at(y, slot, c)] = rst[slot, q]
        accumulate(i, y, c)

    def gather(i):
        slot = zz(OFFSETS[i])
        for index, (yy, cc) in ((0, (y, 1 - c)), (1, (1 - y, c)), (2, (1 - y, 1 - c))):
            j = at(yy, slot, cc)
            remote(rst.at[slot, 0], nc.at[j], r_ssem.at[slot, index], nc_rsem.at[index, slot], chip_mate).wait_recv()
            accumulate(i, yy, cc)

    def await_rows(way):
        for index, role in ((0, q_core), (1, q_chip), (2, q_cross)):
            for part in (2 * way, 2 * way + 1):
                cols = pl.ds(part * (QUARTER // PARTS), QUARTER // PARTS)
                remote(nst.at[0, :, cols], nt.at[role, :, cols], n_ssem.at[index, part], n_rsem.at[index, part], core_mate).wait_recv()

    def partial_sums(way):
        @pl.loop(0, RING // 2)
        def _(i):
            cols = pl.ds(pl.multiple_of(way * RING * 128 + i * 256, 256), 256)
            rows = nt[:, :, cols].reshape(TEAM * ROWS, 256)
            r = lax.dot_general(rows, vt[...].reshape(TEAM * ROWS, VW), (((0,), (0,)), ((), ())), preferred_element_type=F32)
            pblk[way, pl.ds(2 * i, 2)] = r.reshape(2, 128, VW)

    def rs_copy(way, side, sub, s):
        return remote(
            rs_send.at[way, side, s, sub], rs_recv.at[way, side, s, sub], rs_ssem.at[way, side, s, sub],
            rs_rsem.at[way, side, s, sub], right if side == 0 else left)

    def first_step(side, sub):
        return 0 if (sub < SUBS // 2) == (side == 0) else 1

    def rs_step(way, s):
        for fresh in (True, False):
            for sub in range(SUBS):
                for side in range(2):
                    start_at = first_step(side, sub)
                    if s < start_at or (s == start_at) != fresh:
                        continue
                    b = zz(4 - s) if side == 0 else zz(s - 4)
                    v = pblk[way, b, pl.ds(sub * SUBROWS, SUBROWS)]
                    if s > start_at:
                        rs_copy(way, side, sub, s - 1).wait_recv()
                        v += rs_recv[way, side, s - 1, sub].astype(F32)
                    rs_send[way, side, s, sub] = v.astype(BF16)
                    start(rs_copy(way, side, sub, s))

    def vg_copy(way, sub):
        return pltpu.make_async_copy(vgb.at[way, sub], vg_out.at[pl.ds(way * 128 + sub * SUBROWS, SUBROWS)], vg_sem.at[way, sub])

    def rs_end(way):
        for sub in range(SUBS):
            v = pblk[way, z, pl.ds(sub * SUBROWS, SUBROWS)]
            for side in range(2):
                rs_copy(way, side, sub, STEPS - 1).wait_recv()
                v += rs_recv[way, side, STEPS - 1, sub].astype(F32)
            vgb[way, sub] = v
            vg_copy(way, sub).start()

    multiply(0)
    multiply(1)
    multiply(2)
    n_part(2)

    remote(vst, vt.at[q_chip], v_ssem.at[0], v_rsem.at[0], chip_mate).wait_recv()
    start(remote(vt.at[q_chip], vt.at[q_chip], v_ssem.at[2], v_rsem.at[2], core_mate))

    forward(0, 1, 0)
    forward(1, 1, 0)
    gather(0)
    forward(0, 1, 1)
    forward(1, 1, 1)
    multiply(3)
    multiply(4)
    gather(1)
    gather(2)

    forward(0, 2, 0)
    w_arrival(1, 2, 0).wait_recv()
    forward(1, 2, 1)
    w_arrival(0, 2, 1).wait_recv()
    multiply(5)
    multiply(6)

    own_n.wait()
    own_v.wait()
    remote(vst, vt.at[q_core], v_ssem.at[1], v_rsem.at[1], core_mate).wait_recv()
    remote(vst, vt.at[q_cross], v_ssem.at[2], v_rsem.at[2], core_mate).wait_recv()
    await_rows(0)
    partial_sums(0)
    rs_step(0, 0)
    w_arrival(0, 3, 0).wait_recv()
    w_arrival(1, 3, 1).wait_recv()
    multiply(7)
    n_part(3)
    rs_step(0, 1)
    gather(3)
    gather(4)
    gather(5)
    gather(6)
    gather(7)

    mean = jnp.sum(s2[...], axis=1, keepdims=True) / WIDTH
    inv_one = invb[...]
    back_send[...] = inv_one * inv_one * inv_one * mean

    def back_copy():
        return to(back_send, back_recv, b_ssem.at[0], b_rsem.at[0], below_p, early_dev)

    @pl.when(p > 0)
    def _():
        back_copy().start()

    def slots(i):
        return [(i * 4 + yy * 2 + cc, at(yy, zz(OFFSETS[i]), cc)) for yy in range(2) for cc in range(2)]

    def finish(slot, j):
        cols = chunk_cols(j)
        scaled = gf[:, cols].astype(F32) * nc[j].astype(F32)
        v = og[:, cols].astype(F32) + twice(invb) * scaled - xf[:, cols].astype(F32) * twice(back_send)
        fin[slot] = v.astype(BF16)

    def c_copy(slot, j, pipe, dev):
        return to(fin.at[slot], cot_out.at[:, chunk_cols(j)], c_ssem.at[slot], c_rsem.at[slot], pipe, dev)

    def relay_at(slot):
        for group in (VIA_ZERO, VIA_MATE):
            if slot // 4 in group:
                return group.index(slot // 4) * 4 + slot % 4

    def via_zero(slot):
        return slot // 4 in VIA_ZERO

    def rl_copy(slot):
        n = relay_at(slot)
        return to(fin.at[slot], relay.at[n], rl_ssem.at[slot], rl_rsem.at[n], 0 if via_zero(slot) else mid, chip_mate)

    def over_copy(slot):
        n = relay_at(slot)
        return to(relay.at[n], relay.at[8 + n], rl_ssem.at[slot], rl_rsem.at[8 + n], 0, chip_mate)

    def on_copy(slot, j):
        n = relay_at(slot) + (8 if via_zero(slot) else 0)
        return to(relay.at[n], cot_out.at[:, chunk_cols(j)], on_ssem.at[n], c_rsem.at[slot], mid - 1, d if via_zero(slot) else chip_mate)

    @pl.when(p == mid)
    def _():
        for i in (VIA_ZERO[0], VIA_MATE[0], VIA_ZERO[1], VIA_MATE[1]):
            for slot, j in slots(i):
                finish(slot, j)
                rl_copy(slot).start()
        for i in DIRECT:
            for slot, j in slots(i):
                finish(slot, j)

    @pl.when(p != mid)
    def _():
        for i in range(EARLY, RING):
            for slot, j in slots(i):
                finish(slot, j)

                @pl.when(p > 0)
                def _():
                    c_copy(slot, j, below_p, d).start()

    rs_step(0, 2)

    def o_copy(slot, j):
        return pltpu.make_async_copy(ar.at[slot], cot_out.at[:, chunk_cols(j)], o_sem.at[slot])

    def zero_copy(slot, j):
        return pltpu.make_async_copy(relay.at[0], cot_out.at[:, chunk_cols(j)], zero_sem.at[slot])

    @pl.when(p == sections - 1)
    def _():
        relay[0] = jnp.zeros((ROWS, CHUNK), BF16)
        for i in range(RING):
            for slot, j in slots(i):
                zero_copy(slot, j).start()

    def mate_copy(slot, j):
        return to(ar.at[slot], cot_out.at[:, chunk_cols(j)], o_sem.at[slot], c_rsem.at[slot], p, chip_mate)

    def correct(i, finished):
        if i == 0:
            back_copy().wait_recv()
        for yy in range(2):
            x_copy(i, yy).wait_recv()
        for slot, j in slots(i):
            a_copy(slot).wait_recv()
            half_cols = pl.ds((slot % 2) * CHUNK, CHUNK)
            v = ar[slot].astype(F32) - xr[slot // 2, :, half_cols].astype(F32) * twice(back_recv)
            ar[slot] = v.astype(BF16)
            finished(slot, j).start()

    def correct_own(i):
        @pl.when((p < sections - 1) & (p != mid - 1))
        def _():
            correct(i, o_copy)

    def pass_over(i):
        @pl.when(p == 0)
        def _():
            for slot, j in slots(i):
                rl_copy(slot).wait_recv()
                over_copy(slot).start()

    def pass_on(section, i):
        @pl.when(p == section)
        def _():
            for slot, j in slots(i):
                (over_copy(slot) if section == 0 else rl_copy(slot)).wait_recv()
                on_copy(slot, j).start()

    rs_step(0, 3)

    @pl.when(p == mid - 1)
    def _():
        for i in range(EARLY_MID):
            correct(i, mate_copy)

    await_rows(1)

    @pl.when(p == mid)
    def _():
        for i in DIRECT:
            for slot, j in slots(i):
                c_copy(slot, j, below_p, d).start()

    partial_sums(1)
    rs_step(1, 0)
    rs_end(0)
    pass_over(VIA_ZERO[0])
    pass_on(mid, VIA_MATE[0])
    rs_step(1, 1)
    correct_own(0)
    pass_on(0, VIA_ZERO[0])
    rs_step(1, 2)
    pass_over(VIA_ZERO[1])
    pass_on(mid, VIA_MATE[1])
    correct_own(1)
    rs_step(1, 3)
    correct_own(2)
    correct_own(3)
    pass_on(0, VIA_ZERO[1])
    rs_end(1)

    @pl.when(p == sections - 1)
    def _():
        for i in range(RING):
            for slot, j in slots(i):
                zero_copy(slot, j).wait()

    @pl.when((p < sections - 1) & (p != mid - 1))
    def _():
        for i in range(EARLY):
            for slot, j in slots(i):
                o_copy(slot, j).wait()

    @pl.when(p == mid - 1)
    def _():
        for i in range(EARLY_MID):
            for slot, j in slots(i):
                mate_copy(slot, j).wait_send()

    @pl.when(p < sections - 1)
    def _():
        for i in range(EARLY, RING):
            for slot, j in slots(i):
                c_copy(slot, j, below_p, d).wait_recv()

    @pl.when(p == mid - 1)
    def _():
        for i in range(EARLY):
            for slot, j in slots(i):
                c_copy(slot, j, below_p, d).wait_recv()

    @pl.when(p > 0)
    def _():
        back_copy().wait_send()

    for i in range(EARLY):
        @pl.when(sends_early(i))
        def _():
            for yy in range(2):
                x_copy(i, yy).wait_send()
            for slot, j in slots(i):
                a_copy(slot).wait_send()

    @pl.when(p == mid)
    def _():
        for i in VIA_ZERO + VIA_MATE:
            for slot, j in slots(i):
                rl_copy(slot).wait_send()
        for i in VIA_MATE:
            for slot, j in slots(i):
                on_copy(slot, j).wait_send()
        for i in DIRECT:
            for slot, j in slots(i):
                c_copy(slot, j, below_p, d).wait_send()

    @pl.when(p == 0)
    def _():
        for i in VIA_ZERO:
            for slot, j in slots(i):
                over_copy(slot).wait_send()
                on_copy(slot, j).wait_send()

    @pl.when((p > 0) & (p != mid))
    def _():
        for i in range(EARLY, RING):
            for slot, j in slots(i):
                c_copy(slot, j, below_p, d).wait_send()

    for way in range(2):
        for sub in range(SUBS):
            vg_copy(way, sub).wait()
    for copy in sent:
        copy.wait_send()


def place(cot_in, vg_in, cot_out, vg_out, cot, vg, in_sem, out_sem):
    steps = []
    for n in range(PLACES):
        for which, (src, mid, dst) in enumerate(((cot_in, cot, cot_out), (vg_in, vg, vg_out))):
            size = src.shape[0] // PLACES
            rows = pl.ds(n * size, size)
            steps.append((
                pltpu.make_async_copy(src.at[rows], mid.at[rows], in_sem.at[which, n]),
                pltpu.make_async_copy(mid.at[rows], dst.at[rows], out_sem.at[which, n])))
    for take, _ in steps:
        take.start()
    for take, put in steps:
        take.wait()
        put.start()
    for _, put in steps:
        put.wait()


def shards(sections, *args):
    args = [a[0] if a.ndim == 3 else a for a in args]
    any_space = pl.BlockSpec(memory_space=pl.ANY)
    dma = pltpu.SemaphoreType.DMA
    cot, vg = pl.pallas_call(
        functools.partial(kernel, sections),
        out_shape=(
            jax.ShapeDtypeStruct((ROWS, WIDTH), BF16),
            jax.ShapeDtypeStruct((CHUNK, VW), F32),
        ),
        in_specs=[any_space] * 11,
        out_specs=(any_space, any_space),
        scratch_shapes=[
            pltpu.VMEM((ROWS, WIDTH), BF16),
            pltpu.VMEM((1, WIDTH), BF16),
            pltpu.VMEM((ROWS, 4096), BF16),
            pltpu.VMEM((ROWS, VW), BF16),
            pltpu.VMEM((ROWS, 4096), BF16),
            pltpu.VMEM((1, ROWS), jnp.int32),
            pltpu.VMEM((ROWS, WIDTH), BF16),
            pltpu.VMEM((1, WIDTH), BF16),
            pltpu.VMEM((ROWS, WIDTH), BF16),
            pltpu.VMEM((TEAM, ROWS, KW), BF16),
            pltpu.VMEM((RING, CHUNK, KW), BF16),
            pltpu.VMEM((RING, TEAM, ROWS, CHUNK), BF16),
            pltpu.VMEM((CHUNKS, ROWS, CHUNK), BF16),
            pltpu.VMEM((TEAM, ROWS, QUARTER), BF16),
            pltpu.VMEM((TEAM, ROWS, QUARTER), BF16),
            pltpu.VMEM((ROWS, VW), BF16),
            pltpu.VMEM((TEAM, ROWS, VW), BF16),
            pltpu.VMEM((2, RING, 128, VW), F32),
            pltpu.VMEM((2, 2, STEPS, SUBS, SUBROWS, VW), BF16),
            pltpu.VMEM((2, 2, STEPS, SUBS, SUBROWS, VW), BF16),
            pltpu.VMEM((CHUNKS, ROWS, CHUNK), BF16),
            pltpu.VMEM((4 * EARLY, ROWS, CHUNK), BF16),
            pltpu.VMEM((4 * EARLY, ROWS, CHUNK), BF16),
            pltpu.VMEM((2 * EARLY, ROWS, 2 * CHUNK), BF16),
            pltpu.VMEM((4 * EARLY, ROWS, CHUNK), BF16),
            pltpu.VMEM((ROWS, 128), F32),
            pltpu.VMEM((ROWS, 128), F32),
            pltpu.VMEM((ROWS, 128), F32),
            pltpu.VMEM((ROWS, 128), F32),
            pltpu.VMEM((ROWS, 128), F32),
            pltpu.VMEM((2, SUBS, SUBROWS, VW), F32),
            dma((11,)),
            dma((3,)), dma((3,)),
            dma((2, 7)), dma((2, 7)),
            dma((RING, 3)), dma((3, RING)),
            dma((3, PARTS)), dma((3, PARTS)),
            dma((3,)), dma((3,)),
            dma((2, 2, STEPS, SUBS)), dma((2, 2, STEPS, SUBS)),
            dma((CHUNKS,)), dma((CHUNKS,)),
            dma((2 * EARLY,)), dma((2 * EARLY,)),
            dma((4 * EARLY,)), dma((4 * EARLY,)),
            dma((1,)), dma((1,)),
            dma((CHUNKS,)), dma((4 * EARLY,)), dma((4 * EARLY,)),
            dma((2,)),
            dma((4 * EARLY,)), dma((CHUNKS,)), dma((2, SUBS)),
        ],
        compiler_params=pltpu.CompilerParams(
            collective_id=0, has_side_effects=True, vmem_limit_bytes=60 * 1024 * 1024),
        cost_estimate=pl.CostEstimate(flops=6_000_000_000, bytes_accessed=20_000_000, transcendentals=600_000),
    )(*args)
    cot, vg = pl.pallas_call(
        place,
        out_shape=(
            jax.ShapeDtypeStruct((ROWS, WIDTH), BF16),
            jax.ShapeDtypeStruct((CHUNK, VW), F32),
        ),
        in_specs=[any_space] * 2,
        out_specs=(any_space, any_space),
        scratch_shapes=[
            pltpu.VMEM((ROWS, WIDTH), BF16),
            pltpu.VMEM((CHUNK, VW), F32),
            dma((2, PLACES)), dma((2, PLACES)),
        ],
        compiler_params=pltpu.CompilerParams(vmem_limit_bytes=60 * 1024 * 1024),
        cost_estimate=pl.CostEstimate(flops=0, bytes_accessed=5_200_000, transcendentals=0),
    )(cot, vg)
    return cot[None], vg[None]


def solution(mesh):
    placed = (
        P("pipe", "dp", None),
        P("pipe", None),
        P("pipe", "dp", None),
        P("pipe", "dp", None),
        P("pipe", "dp", None),
        P("pipe", "dp"),
        P("pipe", "dp", None),
        P("pipe", None),
        P("pipe", "dp", None),
        P("pipe", "dp", None),
        P("pipe", "dp", None),
    )
    return jax.shard_map(
        functools.partial(shards, mesh.shape["pipe"]),
        mesh=mesh,
        in_specs=placed,
        out_specs=(P("pipe", "dp", None), P("pipe", "dp", None)),
        check_vma=False,
    )
```

```python
import functools
import math

import jax
import jax.numpy as jnp
from jax import lax
from jax.experimental import pallas as pl
from jax.experimental.pallas import tpu as pltpu
from jax.sharding import PartitionSpec as P

HEAD = 128
NORM_EPS = 1e-05
MASKED = -1e30

MESH = pl.DeviceIdType.MESH
F32 = jnp.float32
BF16 = jnp.bfloat16

RING = 8
TEAM = 4
ROWS = 128
WIDTH = 8192
CHUNK = 256
CHUNKS = 32
QUARTER = 2048
VW = 512
KW = 1024
PARTS = 4
SUBS = 4
SUBROWS = 128 // SUBS
STEPS = RING // 2
OFFSETS = (0, -1, 1, -2, 2, -3, 3, 4)
EARLY = 4
EARLY_MID = 3
VIA_ZERO = (3, 6)
VIA_MATE = (4,)
DIRECT = (5, 7)
PLACES = 8


def kernel(
    sections,
    x_new, g_new, q_in, k_in, ctx_in, seg_in, x_frz, g_frz, og_in, kv_in, w_in,
    cot_out, vg_out,
    xn, gn, qv, kk, cx, sg, xf, gf, og, kvt, wbuf, rst, nc, nst, nt, vst, vt,
    pblk, rs_send, rs_recv, fin, ast, ar, xr, relay, back_send, back_recv, invb, s2, sq, vgb,
    load_sem, kv_ssem, kv_rsem, w_ssem, w_rsem, r_ssem, nc_rsem, n_ssem, n_rsem,
    v_ssem, v_rsem, rs_ssem, rs_rsem, c_ssem, c_rsem, x_ssem, x_rsem, a_ssem, a_rsem,
    b_ssem, b_rsem, rl_ssem, rl_rsem, on_ssem, own_sem, o_sem, zero_sem, vg_sem,
):
    p = lax.axis_index("pipe")
    d = lax.axis_index("dp")
    y = d // 16
    z = (d // 2) % RING
    c = d % 2
    q = y * 2 + c

    def at(yy, zz, cc):
        return yy * 16 + zz * 2 + cc

    right = at(y, (z + 1) % RING, c)
    left = at(y, (z + RING - 1) % RING, c)
    core_mate = at(y, z, 1 - c)
    chip_mate = at(1 - y, z, c)
    cross_mate = at(1 - y, z, 1 - c)
    early_dev = jnp.where(p == sections // 2, chip_mate, d)

    def remote(src, dst, ssem, rsem, dev):
        return pltpu.make_async_remote_copy(
            src_ref=src, dst_ref=dst, send_sem=ssem, recv_sem=rsem,
            device_id={"dp": dev}, device_id_type=MESH)

    mid = sections // 2
    below_p = lax.rem(p + sections - 1, sections)

    def sends_early(i):
        return (p > 0) & ((p != mid) | (i < EARLY_MID))

    def to(src, dst, ssem, rsem, pipe, dev):
        return pltpu.make_async_remote_copy(
            src_ref=src, dst_ref=dst, send_sem=ssem, recv_sem=rsem,
            device_id={"pipe": pipe, "dp": dev}, device_id_type=MESH)

    def signal(pipe, dev):
        pl.semaphore_signal(barrier, inc=1, device_id={"pipe": pipe, "dp": dev}, device_id_type=MESH)

    loads = [
        pltpu.make_async_copy(x_new, xn, load_sem.at[0]),
        pltpu.make_async_copy(g_new, gn, load_sem.at[1]),
        pltpu.make_async_copy(seg_in, sg, load_sem.at[2]),
        pltpu.make_async_copy(k_in, kk, load_sem.at[3]),
        pltpu.make_async_copy(q_in, qv, load_sem.at[4]),
        pltpu.make_async_copy(ctx_in, cx, load_sem.at[5]),
        pltpu.make_async_copy(kv_in, kvt.at[q], load_sem.at[6]),
        pltpu.make_async_copy(w_in, wbuf.at[z], load_sem.at[7]),
        pltpu.make_async_copy(x_frz, xf, load_sem.at[8]),
        pltpu.make_async_copy(g_frz, gf, load_sem.at[9]),
        pltpu.make_async_copy(og_in, og, load_sem.at[10]),
    ]
    for load in loads:
        load.start()

    barrier = pltpu.get_barrier_semaphore()
    for dev in (right, left, core_mate, chip_mate, cross_mate):
        pl.semaphore_signal(barrier, inc=1, device_id={"dp": dev}, device_id_type=MESH)

    @pl.when(p > 0)
    def _():
        signal(below_p, d)

    @pl.when(p < sections - 1)
    def _():
        signal(lax.rem(p + 1, sections), d)

    @pl.when(p == mid)
    def _():
        signal(0, chip_mate)
        signal(mid - 1, chip_mate)

    @pl.when(p == 0)
    def _():
        signal(mid, chip_mate)
        signal(mid - 1, d)

    @pl.when(p == mid - 1)
    def _():
        signal(0, d)
        signal(mid, chip_mate)

    pl.semaphore_wait(
        barrier,
        5 + jnp.where(p > 0, 1, 2) + jnp.where(p < sections - 1, 1, 0)
        + jnp.where((p == mid) | (p == mid - 1), 2, 0))

    def half(slot, h):
        return wbuf.at[slot, pl.ds(h * 128, 128)]

    def zz(k):
        return (z + RING + k) % RING

    def w_copy(way, k, h, own=False):
        slot = zz(-k) if way == 0 else zz(k)
        n = 2 * k + (h if k < 3 else 0)
        src = w_in.at[pl.ds(h * 128, 128)] if own else half(slot, h)
        return remote(src, half(slot, h), w_ssem.at[way, n], w_rsem.at[way, n], right if way == 0 else left)

    def w_arrival(way, k, h):
        slot = zz(-(k + 1)) if way == 0 else zz(k + 1)
        n = 2 * k + (h if k < 3 else 0)
        return remote(half(slot, h), half(slot, h), w_ssem.at[way, n], w_rsem.at[way, n], right if way == 0 else left)

    sent = []

    def start(copy):
        copy.start()
        sent.append(copy)

    for h in range(2):
        start(w_copy(0, 0, h, own=True))
        start(w_copy(1, 0, h, own=True))

    start(remote(kv_in, kvt.at[q], kv_ssem.at[0], kv_rsem.at[0], chip_mate))
    start(remote(kv_in, kvt.at[q], kv_ssem.at[1], kv_rsem.at[1], core_mate))

    def chunk_cols(j):
        return pl.ds(pl.multiple_of(j * CHUNK, CHUNK), CHUNK)

    def x_copy(i, yy):
        cols = pl.ds(pl.multiple_of(at(yy, zz(OFFSETS[i]), 0) * CHUNK, 2 * CHUNK), 2 * CHUNK)
        return to(x_frz.at[:, cols], xr.at[i * 2 + yy], x_ssem.at[i * 2 + yy], x_rsem.at[i * 2 + yy], below_p, early_dev)

    for i in range(EARLY):
        @pl.when(sends_early(i))
        def _():
            for yy in range(2):
                x_copy(i, yy).start()

    q_core = y * 2 + (1 - c)
    q_chip = (1 - y) * 2 + c
    q_cross = (1 - y) * 2 + (1 - c)

    loads[0].wait()
    loads[1].wait()
    sq[...] = jnp.zeros_like(sq)

    @pl.loop(0, CHUNKS)
    def _(j):
        v = xn[:, pl.ds(pl.multiple_of(j * CHUNK, CHUNK), CHUNK)].astype(F32)
        v = v * v
        sq[...] += v[:, :128] + v[:, 128:]

    inv_new = lax.rsqrt(jnp.sum(sq[...], axis=1, keepdims=True) / WIDTH + NORM_EPS)

    @pl.loop(0, CHUNKS)
    def _(j):
        cols = pl.ds(pl.multiple_of(j * CHUNK, CHUNK), CHUNK)
        v = xn[:, cols].astype(F32) * inv_new * gn[:, cols].astype(F32)
        role = (j // 16) * 2 + j % 2
        block = ((j // 2) % RING) * 128
        v = v.astype(BF16)
        nst[role, :, pl.ds(pl.multiple_of(block, 128), 128)] = v[:, :128]
        nst[role, :, pl.ds(pl.multiple_of(block + RING * 128, 128), 128)] = v[:, 128:]

    def n_copy(index, role, dev, part):
        cols = pl.ds(part * (QUARTER // PARTS), QUARTER // PARTS)
        return remote(nst.at[role, :, cols], nt.at[q, :, cols], n_ssem.at[index, part], n_rsem.at[index, part], dev)

    def n_part(part):
        start(n_copy(1, q_chip, chip_mate, part))
        start(n_copy(2, q_cross, cross_mate, part))

    own_n = pltpu.make_async_copy(nst.at[q], nt.at[q], own_sem.at[0])
    own_n.start()
    n_part(0)
    for part in range(PARTS):
        start(n_copy(0, q_core, core_mate, part))

    def forward(way, k, h):
        w_arrival(way, k, h).wait_recv()
        start(w_copy(way, k + 1, h))

    n_part(1)

    forward(0, 0, 0)
    forward(1, 0, 0)

    remote(kv_in, kvt.at[q_chip], kv_ssem.at[0], kv_rsem.at[0], chip_mate).wait_recv()
    start(remote(kvt.at[q_chip], kvt.at[q_chip], kv_ssem.at[2], kv_rsem.at[2], core_mate))

    for load in loads[2:6]:
        load.wait()
    seg_i = jnp.broadcast_to(sg[...].astype(F32), (ROWS, ROWS))
    seg_j = seg_i.T
    pos_j = lax.broadcasted_iota(jnp.int32, (ROWS, ROWS), 0)
    pos_i = lax.broadcasted_iota(jnp.int32, (ROWS, ROWS), 1)
    visible_one = jnp.where((seg_i == seg_j) & (pos_j <= pos_i), 1.0, 0.0)
    scale = 1.0 / math.sqrt(HEAD)

    @pl.loop(0, 4)
    def _(g):
        keys = kk[:, pl.ds(pl.multiple_of(g * HEAD, HEAD), HEAD)]
        total = jnp.zeros((ROWS, HEAD), F32)
        for h in range(8):
            cols = pl.ds(pl.multiple_of(g * 8 * HEAD + h * HEAD, HEAD), HEAD)
            s = lax.dot_general(keys, qv[:, cols], (((1,), (1,)), ((), ())), preferred_element_type=F32) * scale
            seen = visible_one > 0.5
            s = jnp.where(seen, s, MASKED)
            top = jnp.max(s, axis=0, keepdims=True)
            e = jnp.where(seen, jnp.exp(s - top), 0.0)
            a = (e / jnp.sum(e, axis=0, keepdims=True)).astype(BF16)
            total += jnp.dot(a, cx[:, cols], preferred_element_type=F32)
        vst[:, pl.ds(pl.multiple_of(g * HEAD, HEAD), HEAD)] = total.astype(BF16)

    start(remote(vst, vt.at[q], v_ssem.at[0], v_rsem.at[0], chip_mate))
    start(remote(vst, vt.at[q], v_ssem.at[1], v_rsem.at[1], core_mate))
    own_v = pltpu.make_async_copy(vst, vt.at[q], own_sem.at[1])
    own_v.start()

    forward(0, 0, 1)
    forward(1, 0, 1)

    for load in loads[6:11]:
        load.wait()
    remote(kv_in, kvt.at[q_core], kv_ssem.at[1], kv_rsem.at[1], core_mate).wait_recv()
    remote(kv_in, kvt.at[q_cross], kv_ssem.at[2], kv_rsem.at[2], core_mate).wait_recv()

    s2[...] = jnp.zeros_like(s2)
    sq[...] = jnp.zeros_like(sq)

    @pl.loop(0, CHUNKS)
    def _(j):
        v = xf[:, chunk_cols(j)].astype(F32)
        v = v * v
        sq[...] += v[:, :128] + v[:, 128:]

    inv_frz = lax.rsqrt(jnp.sum(sq[...], axis=1, keepdims=True) / WIDTH + NORM_EPS)
    invb[...] = jnp.broadcast_to(inv_frz, (ROWS, 128))

    def twice(ref):
        v = ref[...]
        return jnp.concatenate([v, v], axis=1)

    def a_copy(slot):
        return to(ast.at[slot], ar.at[slot], a_ssem.at[slot], a_rsem.at[slot], below_p, early_dev)

    def accumulate(i, yy, cc):
        j = at(yy, zz(OFFSETS[i]), cc)
        cols = chunk_cols(j)
        scaled = gf[:, cols].astype(F32) * nc[j].astype(F32)
        v = xf[:, cols].astype(F32) * scaled
        s2[...] += v[:, :128] + v[:, 128:]
        if i < EARLY:
            slot = i * 4 + yy * 2 + cc
            ast[slot] = (og[:, cols].astype(F32) + twice(invb) * scaled).astype(BF16)

            @pl.when(sends_early(i))
            def _():
                a_copy(slot).start()

    def result_copy(slot, index, role, dev):
        j = at(y, slot, c)
        return remote(rst.at[slot, role], nc.at[j], r_ssem.at[slot, index], nc_rsem.at[index, slot], dev)

    def multiply(i):
        slot = zz(OFFSETS[i])
        w = wbuf[slot]
        for m in range(2):
            kv = kvt[pl.ds(2 * m, 2)].reshape(2 * ROWS, KW)
            r = lax.dot_general(kv, w, (((1,), (1,)), ((), ())), preferred_element_type=F32)
            rst[slot, pl.ds(2 * m, 2)] = r.astype(BF16).reshape(2, ROWS, CHUNK)
        start(result_copy(slot, 1, q_chip, chip_mate))
        start(result_copy(slot, 2, q_cross, cross_mate))
        start(result_copy(slot, 0, q_core, core_mate))
        nc[at(y, slot, c)] = rst[slot, q]
        accumulate(i, y, c)

    def gather(i):
        slot = zz(OFFSETS[i])
        for index, (yy, cc) in ((0, (y, 1 - c)), (1, (1 - y, c)), (2, (1 - y, 1 - c))):
            j = at(yy, slot, cc)
            remote(rst.at[slot, 0], nc.at[j], r_ssem.at[slot, index], nc_rsem.at[index, slot], chip_mate).wait_recv()
            accumulate(i, yy, cc)

    def await_rows(way):
        for index, role in ((0, q_core), (1, q_chip), (2, q_cross)):
            for part in (2 * way, 2 * way + 1):
                cols = pl.ds(part * (QUARTER // PARTS), QUARTER // PARTS)
                remote(nst.at[0, :, cols], nt.at[role, :, cols], n_ssem.at[index, part], n_rsem.at[index, part], core_mate).wait_recv()

    def partial_sums(way, begin, end):
        @pl.loop(begin, end)
        def _(n):
            i = ((z + RING // 2) // 2 + n) % (RING // 2)
            cols = pl.ds(pl.multiple_of(way * RING * 128 + i * 256, 256), 256)
            rows = nt[:, :, cols].reshape(TEAM * ROWS, 256)
            r = lax.dot_general(rows, vt[...].reshape(TEAM * ROWS, VW), (((0,), (0,)), ((), ())), preferred_element_type=F32)
            pblk[way, pl.ds(2 * i, 2)] = r.reshape(2, 128, VW)

    def rs_copy(way, side, sub, s):
        return remote(
            rs_send.at[way, side, s, sub], rs_recv.at[way, side, s, sub], rs_ssem.at[way, side, s, sub],
            rs_rsem.at[way, side, s, sub], right if side == 0 else left)

    def first_step(side, sub):
        return 0 if (sub < SUBS // 2) == (side == 0) else 1

    def rs_step(way, s):
        for fresh in (True, False):
            for sub in range(SUBS):
                for side in range(2):
                    start_at = first_step(side, sub)
                    if s < start_at or (s == start_at) != fresh:
                        continue
                    b = zz(4 - s) if side == 0 else zz(s - 4)
                    v = pblk[way, b, pl.ds(sub * SUBROWS, SUBROWS)]
                    if s > start_at:
                        rs_copy(way, side, sub, s - 1).wait_recv()
                        v += rs_recv[way, side, s - 1, sub].astype(F32)
                    rs_send[way, side, s, sub] = v.astype(BF16)
                    start(rs_copy(way, side, sub, s))

    def vg_copy(way, sub):
        return pltpu.make_async_copy(vgb.at[way, sub], vg_out.at[pl.ds(way * 128 + sub * SUBROWS, SUBROWS)], vg_sem.at[way, sub])

    def rs_end(way):
        for sub in range(SUBS):
            v = pblk[way, z, pl.ds(sub * SUBROWS, SUBROWS)]
            for side in range(2):
                rs_copy(way, side, sub, STEPS - 1).wait_recv()
                v += rs_recv[way, side, STEPS - 1, sub].astype(F32)
            vgb[way, sub] = v
            vg_copy(way, sub).start()

    multiply(0)
    multiply(1)
    multiply(2)

    remote(vst, vt.at[q_chip], v_ssem.at[0], v_rsem.at[0], chip_mate).wait_recv()
    start(remote(vt.at[q_chip], vt.at[q_chip], v_ssem.at[2], v_rsem.at[2], core_mate))

    forward(0, 1, 0)
    forward(1, 1, 0)
    gather(0)
    forward(0, 1, 1)
    forward(1, 1, 1)
    multiply(3)
    multiply(4)
    gather(1)
    gather(2)

    forward(0, 2, 0)
    w_arrival(1, 2, 0).wait_recv()
    forward(1, 2, 1)
    w_arrival(0, 2, 1).wait_recv()
    multiply(5)
    multiply(6)

    own_n.wait()
    own_v.wait()
    remote(vst, vt.at[q_core], v_ssem.at[1], v_rsem.at[1], core_mate).wait_recv()
    remote(vst, vt.at[q_cross], v_ssem.at[2], v_rsem.at[2], core_mate).wait_recv()
    await_rows(0)
    partial_sums(0, 0, 1)
    rs_step(0, 0)
    w_arrival(0, 3, 0).wait_recv()
    w_arrival(1, 3, 1).wait_recv()
    multiply(7)
    n_part(2)
    n_part(3)
    partial_sums(0, 1, RING // 2)
    rs_step(0, 1)
    gather(3)
    gather(4)
    gather(5)
    gather(6)
    gather(7)

    mean = jnp.sum(s2[...], axis=1, keepdims=True) / WIDTH
    inv_one = invb[...]
    back_send[...] = inv_one * inv_one * inv_one * mean

    def back_copy():
        return to(back_send, back_recv, b_ssem.at[0], b_rsem.at[0], below_p, early_dev)

    @pl.when(p > 0)
    def _():
        back_copy().start()

    def slots(i):
        return [(i * 4 + yy * 2 + cc, at(yy, zz(OFFSETS[i]), cc)) for yy in range(2) for cc in range(2)]

    def finish(slot, j):
        cols = chunk_cols(j)
        scaled = gf[:, cols].astype(F32) * nc[j].astype(F32)
        v = og[:, cols].astype(F32) + twice(invb) * scaled - xf[:, cols].astype(F32) * twice(back_send)
        fin[slot] = v.astype(BF16)

    def c_copy(slot, j, pipe, dev):
        return to(fin.at[slot], cot_out.at[:, chunk_cols(j)], c_ssem.at[slot], c_rsem.at[slot], pipe, dev)

    def relay_at(slot):
        for group in (VIA_ZERO, VIA_MATE):
            if slot // 4 in group:
                return group.index(slot // 4) * 4 + slot % 4

    def via_zero(slot):
        return slot // 4 in VIA_ZERO

    def rl_copy(slot):
        n = relay_at(slot)
        return to(fin.at[slot], relay.at[n], rl_ssem.at[slot], rl_rsem.at[n], 0 if via_zero(slot) else mid, chip_mate)

    def over_copy(slot):
        n = relay_at(slot)
        return to(relay.at[n], relay.at[8 + n], rl_ssem.at[slot], rl_rsem.at[8 + n], 0, chip_mate)

    def on_copy(slot, j):
        n = relay_at(slot) + (8 if via_zero(slot) else 0)
        return to(relay.at[n], cot_out.at[:, chunk_cols(j)], on_ssem.at[n], c_rsem.at[slot], mid - 1, d if via_zero(slot) else chip_mate)

    @pl.when(p == mid)
    def _():
        for i in VIA_ZERO + VIA_MATE:
            for slot, j in slots(i):
                finish(slot, j)
                rl_copy(slot).start()
        for i in DIRECT:
            for slot, j in slots(i):
                finish(slot, j)

    @pl.when(p != mid)
    def _():
        for i in range(EARLY, RING):
            for slot, j in slots(i):
                finish(slot, j)

                @pl.when(p > 0)
                def _():
                    c_copy(slot, j, below_p, d).start()

    rs_step(0, 2)

    def o_copy(slot, j):
        return pltpu.make_async_copy(ar.at[slot], cot_out.at[:, chunk_cols(j)], o_sem.at[slot])

    def zero_copy(slot, j):
        return pltpu.make_async_copy(relay.at[0], cot_out.at[:, chunk_cols(j)], zero_sem.at[slot])

    @pl.when(p == sections - 1)
    def _():
        relay[0] = jnp.zeros((ROWS, CHUNK), BF16)
        for i in range(RING):
            for slot, j in slots(i):
                zero_copy(slot, j).start()

    def mate_copy(slot, j):
        return to(ar.at[slot], cot_out.at[:, chunk_cols(j)], o_sem.at[slot], c_rsem.at[slot], p, chip_mate)

    def correct(i, finished):
        if i == 0:
            back_copy().wait_recv()
        for yy in range(2):
            x_copy(i, yy).wait_recv()
        for slot, j in slots(i):
            a_copy(slot).wait_recv()
            half_cols = pl.ds((slot % 2) * CHUNK, CHUNK)
            v = ar[slot].astype(F32) - xr[slot // 2, :, half_cols].astype(F32) * twice(back_recv)
            ar[slot] = v.astype(BF16)
            finished(slot, j).start()

    def correct_own(i):
        @pl.when((p < sections - 1) & (p != mid - 1))
        def _():
            correct(i, o_copy)

    def pass_over(i):
        @pl.when(p == 0)
        def _():
            for slot, j in slots(i):
                rl_copy(slot).wait_recv()
                over_copy(slot).start()

    def pass_on(section, i):
        @pl.when(p == section)
        def _():
            for slot, j in slots(i):
                (over_copy(slot) if section == 0 else rl_copy(slot)).wait_recv()
                on_copy(slot, j).start()

    rs_step(0, 3)

    @pl.when(p == mid - 1)
    def _():
        for i in range(EARLY_MID):
            correct(i, mate_copy)

    await_rows(1)

    @pl.when(p == mid)
    def _():
        for i in DIRECT:
            for slot, j in slots(i):
                c_copy(slot, j, below_p, d).start()

    partial_sums(1, 0, 1)
    rs_step(1, 0)
    partial_sums(1, 1, RING // 2)
    rs_end(0)
    pass_over(VIA_ZERO[0])
    pass_on(mid, VIA_MATE[0])
    rs_step(1, 1)
    correct_own(0)
    pass_on(0, VIA_ZERO[0])
    rs_step(1, 2)
    pass_over(VIA_ZERO[1])
    correct_own(1)
    rs_step(1, 3)
    pass_on(0, VIA_ZERO[1])
    correct_own(2)
    correct_own(3)
    rs_end(1)

    @pl.when(p == sections - 1)
    def _():
        for i in range(RING):
            for slot, j in slots(i):
                zero_copy(slot, j).wait()

    @pl.when((p < sections - 1) & (p != mid - 1))
    def _():
        for i in range(EARLY):
            for slot, j in slots(i):
                o_copy(slot, j).wait()

    @pl.when(p == mid - 1)
    def _():
        for i in range(EARLY_MID):
            for slot, j in slots(i):
                mate_copy(slot, j).wait_send()

    @pl.when(p < sections - 1)
    def _():
        for i in range(EARLY, RING):
            for slot, j in slots(i):
                c_copy(slot, j, below_p, d).wait_recv()

    @pl.when(p == mid - 1)
    def _():
        for i in range(EARLY):
            for slot, j in slots(i):
                c_copy(slot, j, below_p, d).wait_recv()

    @pl.when(p > 0)
    def _():
        back_copy().wait_send()

    for i in range(EARLY):
        @pl.when(sends_early(i))
        def _():
            for yy in range(2):
                x_copy(i, yy).wait_send()
            for slot, j in slots(i):
                a_copy(slot).wait_send()

    @pl.when(p == mid)
    def _():
        for i in VIA_ZERO + VIA_MATE:
            for slot, j in slots(i):
                rl_copy(slot).wait_send()
        for i in VIA_MATE:
            for slot, j in slots(i):
                on_copy(slot, j).wait_send()
        for i in DIRECT:
            for slot, j in slots(i):
                c_copy(slot, j, below_p, d).wait_send()

    @pl.when(p == 0)
    def _():
        for i in VIA_ZERO:
            for slot, j in slots(i):
                over_copy(slot).wait_send()
                on_copy(slot, j).wait_send()

    @pl.when((p > 0) & (p != mid))
    def _():
        for i in range(EARLY, RING):
            for slot, j in slots(i):
                c_copy(slot, j, below_p, d).wait_send()

    for way in range(2):
        for sub in range(SUBS):
            vg_copy(way, sub).wait()
    for copy in sent:
        copy.wait_send()


def place(cot_in, vg_in, cot_out, vg_out, cot, vg, in_sem, out_sem):
    steps = []
    for n in range(PLACES):
        for which, (src, mid, dst) in enumerate(((cot_in, cot, cot_out), (vg_in, vg, vg_out))):
            size = src.shape[0] // PLACES
            rows = pl.ds(n * size, size)
            steps.append((
                pltpu.make_async_copy(src.at[rows], mid.at[rows], in_sem.at[which, n]),
                pltpu.make_async_copy(mid.at[rows], dst.at[rows], out_sem.at[which, n])))
    for take, _ in steps:
        take.start()
    for take, put in steps:
        take.wait()
        put.start()
    for _, put in steps:
        put.wait()


def shards(sections, *args):
    args = [a[0] if a.ndim == 3 else a for a in args]
    any_space = pl.BlockSpec(memory_space=pl.ANY)
    dma = pltpu.SemaphoreType.DMA
    cot, vg = pl.pallas_call(
        functools.partial(kernel, sections),
        out_shape=(
            jax.ShapeDtypeStruct((ROWS, WIDTH), BF16),
            jax.ShapeDtypeStruct((CHUNK, VW), F32),
        ),
        in_specs=[any_space] * 11,
        out_specs=(any_space, any_space),
        scratch_shapes=[
            pltpu.VMEM((ROWS, WIDTH), BF16),
            pltpu.VMEM((1, WIDTH), BF16),
            pltpu.VMEM((ROWS, 4096), BF16),
            pltpu.VMEM((ROWS, VW), BF16),
            pltpu.VMEM((ROWS, 4096), BF16),
            pltpu.VMEM((1, ROWS), jnp.int32),
            pltpu.VMEM((ROWS, WIDTH), BF16),
            pltpu.VMEM((1, WIDTH), BF16),
            pltpu.VMEM((ROWS, WIDTH), BF16),
            pltpu.VMEM((TEAM, ROWS, KW), BF16),
            pltpu.VMEM((RING, CHUNK, KW), BF16),
            pltpu.VMEM((RING, TEAM, ROWS, CHUNK), BF16),
            pltpu.VMEM((CHUNKS, ROWS, CHUNK), BF16),
            pltpu.VMEM((TEAM, ROWS, QUARTER), BF16),
            pltpu.VMEM((TEAM, ROWS, QUARTER), BF16),
            pltpu.VMEM((ROWS, VW), BF16),
            pltpu.VMEM((TEAM, ROWS, VW), BF16),
            pltpu.VMEM((2, RING, 128, VW), F32),
            pltpu.VMEM((2, 2, STEPS, SUBS, SUBROWS, VW), BF16),
            pltpu.VMEM((2, 2, STEPS, SUBS, SUBROWS, VW), BF16),
            pltpu.VMEM((CHUNKS, ROWS, CHUNK), BF16),
            pltpu.VMEM((4 * EARLY, ROWS, CHUNK), BF16),
            pltpu.VMEM((4 * EARLY, ROWS, CHUNK), BF16),
            pltpu.VMEM((2 * EARLY, ROWS, 2 * CHUNK), BF16),
            pltpu.VMEM((4 * EARLY, ROWS, CHUNK), BF16),
            pltpu.VMEM((ROWS, 128), F32),
            pltpu.VMEM((ROWS, 128), F32),
            pltpu.VMEM((ROWS, 128), F32),
            pltpu.VMEM((ROWS, 128), F32),
            pltpu.VMEM((ROWS, 128), F32),
            pltpu.VMEM((2, SUBS, SUBROWS, VW), F32),
            dma((11,)),
            dma((3,)), dma((3,)),
            dma((2, 7)), dma((2, 7)),
            dma((RING, 3)), dma((3, RING)),
            dma((3, PARTS)), dma((3, PARTS)),
            dma((3,)), dma((3,)),
            dma((2, 2, STEPS, SUBS)), dma((2, 2, STEPS, SUBS)),
            dma((CHUNKS,)), dma((CHUNKS,)),
            dma((2 * EARLY,)), dma((2 * EARLY,)),
            dma((4 * EARLY,)), dma((4 * EARLY,)),
            dma((1,)), dma((1,)),
            dma((CHUNKS,)), dma((4 * EARLY,)), dma((4 * EARLY,)),
            dma((2,)),
            dma((4 * EARLY,)), dma((CHUNKS,)), dma((2, SUBS)),
        ],
        compiler_params=pltpu.CompilerParams(
            collective_id=0, has_side_effects=True, vmem_limit_bytes=60 * 1024 * 1024),
        cost_estimate=pl.CostEstimate(flops=6_000_000_000, bytes_accessed=20_000_000, transcendentals=600_000),
    )(*args)
    cot, vg = pl.pallas_call(
        place,
        out_shape=(
            jax.ShapeDtypeStruct((ROWS, WIDTH), BF16),
            jax.ShapeDtypeStruct((CHUNK, VW), F32),
        ),
        in_specs=[any_space] * 2,
        out_specs=(any_space, any_space),
        scratch_shapes=[
            pltpu.VMEM((ROWS, WIDTH), BF16),
            pltpu.VMEM((CHUNK, VW), F32),
            dma((2, PLACES)), dma((2, PLACES)),
        ],
        compiler_params=pltpu.CompilerParams(vmem_limit_bytes=60 * 1024 * 1024),
        cost_estimate=pl.CostEstimate(flops=0, bytes_accessed=5_200_000, transcendentals=0),
    )(cot, vg)
    return cot[None], vg[None]


def solution(mesh):
    placed = (
        P("pipe", "dp", None),
        P("pipe", None),
        P("pipe", "dp", None),
        P("pipe", "dp", None),
        P("pipe", "dp", None),
        P("pipe", "dp"),
        P("pipe", "dp", None),
        P("pipe", None),
        P("pipe", "dp", None),
        P("pipe", "dp", None),
        P("pipe", "dp", None),
    )
    return jax.shard_map(
        functools.partial(shards, mesh.shape["pipe"]),
        mesh=mesh,
        in_specs=placed,
        out_specs=(P("pipe", "dp", None), P("pipe", "dp", None)),
        check_vma=False,
    )
```
